32 devices in a mesh: cfg: 2 (over core), seq: 8 (over z, x), tile: 2 (over y).
Axes of the slice: x: 2, y: 2, z: 4, core: 2. Of those that a mesh axis runs over, the one named last changes fastest.
Arguments:
- section_input: bfloat16 [4, 128, 64, 384], P('tile', None, 'seq'), may hold values from -6 to 6
- norm_gain: float32 [384], replicated, may hold values from 0.5 to 1.5
- conv_weight: bfloat16 [384, 864], replicated, may hold values from -0.0625 to 0.0625
- conv_bias: float32 [32], replicated, may hold values from -3 to 3
- mean_weight: float32 [32, 16], replicated, may hold values from -1 to 1
- mean_bias: float32 [16], replicated, may hold values from -3 to 3
- noisy_tokens: bfloat16 [8192, 64], P(('seq', 'tile')), may hold values from -6 to 6
- mask_tokens: bfloat16 [8192, 128], P(('seq', 'tile')), may hold values from 0 to 1
- patch_weight: bfloat16 [64, 5120], replicated, may hold values from -0.75 to 0.75
- patch_bias: float32 [5120], replicated, may hold values from -3 to 3
- context_weight: bfloat16 [192, 5120], replicated, may hold values from -0.4375 to 0.4375
- context_bias: float32 [5120], replicated, may hold values from -3 to 3
- norm_shift: float32 [5120], replicated, may hold values from -3 to 3
- norm_scale: float32 [5120], replicated, may hold values from -3 to 3
Outputs:
- block_input: bfloat16 [8192, 5120], P(('seq', 'tile'))
The draws below stay inside these ranges and needn't reach their ends.
All inputs are finite; a program needn't handle non-finite values.
Results may differ from the reference program's by a relative error of at most 0.004.
Values may be sent and summed in bfloat16 or wider, within the bound.
A program may use at most 128 MiB of HBM per device.

```python
import jax
import jax.numpy as jnp
from jax import lax

D = 5120
C = 384
Z = 16
MC = 32
K = 3
H = 128
ZO = 32
F = 4
W = 64
S = 8192
N_SEQ = 8
N_TILE = 2


def block_scale(rng, shape, shards, least, top_value):
    loudness, own = 1.0, jax.random.fold_in(rng, 6)
    for axis_at, shards_of in shards:
        draws = jnp.exp(jax.random.uniform(jax.random.fold_in(own, axis_at), (shards_of,), jnp.float32, least / len(shards), top_value / len(shards)))
        loudness = loudness * jnp.repeat(draws, shape[axis_at] // shards_of).reshape([-1 if axis == axis_at else 1 for axis in range(len(shape))])
    return loudness


def noise(key, shape, scale, most, split=(), dtype=jnp.bfloat16):
    entries = scale * jax.random.normal(key, shape, jnp.float32)
    if split:
        entries = entries * block_scale(key, shape, split, -0.22, 0.18)
    return jnp.clip(entries, -most, most).astype(dtype)


def setup_inputs(seed: int = 0) -> dict:
    key_of = jax.random.split(jax.random.key(seed), 15)
    return {
        "section_input": noise(key_of[0], (F, H, W, C), 1.0, 6.0, ((0, 2), (2, 8))),
        "norm_gain": jnp.clip(jax.random.uniform(key_of[1], (C,), jnp.float32, 0.5, 1.5), 0.5, 1.5),
        "conv_weight": noise(key_of[2], (C, K * K * K * ZO), (K * K * K * C) ** -0.5, 0.0625),
        "conv_bias": noise(key_of[3], (ZO,), 0.5, 3.0, (), jnp.float32),
        "mean_weight": noise(key_of[4], (ZO, Z), ZO ** -0.5, 1.0, (), jnp.float32),
        "mean_bias": noise(key_of[5], (Z,), 0.5, 3.0, (), jnp.float32),
        "noisy_tokens": noise(key_of[6], (S, 4 * Z), 1.0, 6.0, ((0, 16),)),
        "mask_tokens": jnp.clip(1.0 * jax.random.uniform(key_of[7], (S, 4 * MC), jnp.float32) ** block_scale(key_of[7], (S, 4 * MC), ((0, 16),), -0.2, 0.2), 0.0, 1.0).astype(jnp.bfloat16),
        "patch_weight": noise(key_of[8], (4 * Z, D), (4 * Z) ** -0.5, 0.75),
        "patch_bias": noise(key_of[9], (D,), 0.5, 3.0, (), jnp.float32),
        "context_weight": noise(key_of[10], (4 * Z + 4 * MC, D), (4 * Z + 4 * MC) ** -0.5, 0.4375),
        "context_bias": noise(key_of[11], (D,), 0.5, 3.0, (), jnp.float32),
        "norm_shift": noise(key_of[12], (D,), 0.5, 3.0, (), jnp.float32),
        "norm_scale": noise(key_of[13], (D,), 0.5, 3.0, (), jnp.float32),
    }


def reference(section_input, norm_gain, conv_weight, conv_bias, mean_weight, mean_bias, noisy_tokens, mask_tokens, patch_weight, patch_bias, context_weight, context_bias, norm_shift, norm_scale):
    frames, height, columns, channels = section_input.shape
    values = section_input.astype(jnp.float32)
    energy = lax.optimization_barrier(jnp.mean(values * values, axis=-1, keepdims=True))
    activation = jax.nn.silu(values * lax.rsqrt(energy + 1e-06) * norm_gain).astype(jnp.bfloat16)
    padded = jnp.pad(activation, ((2, 0), (1, 1), (1, 1), (0, 0)))
    kernel = conv_weight.reshape(channels, K, K, K, -1)
    out_chans = kernel.shape[-1]
    convolved = jnp.zeros((frames * height * columns, out_chans), jnp.float32)
    for step_t in range(K):
        for step_h in range(K):
            for step_w in range(K):
                window = padded[step_t:step_t + frames, step_h:step_h + height, step_w:step_w + columns]
                convolved = convolved + jnp.dot(window.reshape(-1, channels), kernel[:, step_t, step_h, step_w], preferred_element_type=jnp.float32)
    convolved = convolved + conv_bias
    latent = (jnp.dot(convolved, mean_weight, precision=lax.Precision.HIGHEST) + mean_bias).astype(jnp.bfloat16)
    latent_dim = latent.shape[-1]
    latent = latent.reshape(frames, height // 2, 2, columns // 2, 2, latent_dim)
    latent_tokens = latent.transpose(0, 1, 3, 5, 2, 4).reshape(-1, 4 * latent_dim)
    blocks = N_SEQ * N_TILE
    split_at = 4 * latent_dim

    def embed_block(pieces):
        own_latent, own_noise, own_mask = pieces
        main_part = jnp.dot(own_noise, patch_weight, preferred_element_type=jnp.float32) + patch_bias
        context_part = jnp.dot(own_latent, context_weight[:split_at], preferred_element_type=jnp.float32)
        context_part = context_part + jnp.dot(own_mask, context_weight[split_at:], preferred_element_type=jnp.float32) + context_bias
        combined = main_part + context_part
        centred = combined - lax.optimization_barrier(jnp.mean(combined, axis=-1, keepdims=True))
        variance = lax.optimization_barrier(jnp.mean(centred * centred, axis=-1, keepdims=True))
        return (centred * lax.rsqrt(variance + 1e-06) * (1.0 + norm_scale) + norm_shift).astype(jnp.bfloat16)
    result = lax.map(embed_block, (latent_tokens.reshape(blocks, -1, split_at), noisy_tokens.reshape(blocks, -1, noisy_tokens.shape[-1]), mask_tokens.reshape(blocks, -1, mask_tokens.shape[-1])))
    return result.reshape(-1, result.shape[-1])
```

```python
import functools

import jax
import jax.numpy as jnp
from jax import lax
from jax.experimental import pallas as pl
from jax.experimental.pallas import tpu as pltpu
from jax.sharding import PartitionSpec as P

K = 3
MESH = pl.DeviceIdType.MESH
F32 = jnp.float32
BF16 = jnp.bfloat16


def ones_where(shape, test):
    i = lax.broadcasted_iota(jnp.int32, shape, 0)
    j = lax.broadcasted_iota(jnp.int32, shape, 1)
    return jnp.where(test(i, j), 1.0, 0.0)


def nt(x, y):
    return lax.dot_general(x, y, (((1,), (1,)), ((), ())), preferred_element_type=F32)


def fold_weights(cw_ref, mw_ref, wt):
    z, zo = mw_ref.shape
    mw = mw_ref[...]
    high = mw.astype(BF16)
    low = (mw - high.astype(F32)).astype(BF16)
    spread = ones_where((4 * z, z), lambda i, j: i % z == j).astype(BF16)
    copier = ones_where((zo, K * zo), lambda i, j: j % zo == i).astype(BF16)

    def right_slot(i, j):
        slot, e = i // z, j // zo
        return ((slot == 0) & (e == 1)) | ((slot == 2) & (e == 0)) | ((slot == 3) & (e == 2))

    keep = ones_where((4 * z, K * zo), right_slot)
    parts = []
    for part in (high, low):
        tall = jnp.dot(spread, part, preferred_element_type=F32).astype(BF16)
        parts.append((jnp.dot(tall, copier, preferred_element_type=F32) * keep).astype(BF16))
    parts = jnp.concatenate(parts, axis=0)
    nothing = jnp.zeros((z, wt.shape[2]), BF16)
    for a in range(K):
        for b in range(K):
            at = (a * K + b) * K * zo
            rhs = cw_ref[at : at + K * zo, :]
            res = jnp.dot(parts, rhs, preferred_element_type=F32)
            res = (res[: 4 * z] + res[4 * z :]).astype(BF16)
            for f in range(2):
                for slot in range(4):
                    row = slot * 4 * z + (f + 2 - a) * z
                    wt[f * K + b, row : row + z, :] = res[slot * z : (slot + 1) * z]
    for b in range(K):
        for slot in range(4):
            row = slot * 4 * z
            wt[b, row + 3 * z : row + 4 * z, :] = nothing
            wt[K + b, row : row + z, :] = nothing


def fold_bias(mw_ref, cb_ref, mb_ref):
    z = mw_ref.shape[0]
    copier = ones_where((128, z), lambda i, j: i % z == j)
    exact = functools.partial(
        lax.dot_general, dimension_numbers=(((1,), (1,)), ((), ())),
        precision=lax.Precision.HIGHEST, preferred_element_type=F32,
    )
    return exact(exact(cb_ref[...], mw_ref[...]) + mb_ref[...], copier)


def head_kernel(
    sizes, x_hbm, cw_ref, gain_ref, mw_ref, cb_ref, mb_ref, out_ref,
    wt, xin, actf, acc, edge, pk, rs_send, ls_send, ca_send, rs_got, ls_got, ca_got, patch,
    in_sem, s1_sem, r1_sem, s2_sem, r2_sem,
):
    n_c, n_s, n_t, shard_rows = sizes
    c, s, t = lax.axis_index("cfg"), lax.axis_index("seq"), lax.axis_index("tile")
    frames, height, columns, channels = x_hbm.shape
    half = height // n_c
    pairs = half // 2
    z = 16
    chunks = pairs // shard_rows
    chunk_tokens = shard_rows * (columns // 2)

    def dev(ci, si, ti):
        return {"cfg": ci, "seq": si, "tile": ti}

    load = pltpu.make_async_copy(
        x_hbm.at[:, pl.ds(c * (half - 1), half + 1)],
        xin.at[:, pl.ds(1 - c, half + 1)],
        in_sem,
    )
    load.start()

    barrier = pltpu.get_barrier_semaphore()
    links = [(1, 0), (-1, 0), (0, 1), (1, 1), (-1, 1)]

    def there(ds, dt, sign):
        si, ti = s + sign * ds, t + sign * dt
        return (si >= 0) & (si < n_s) & (ti >= 0) & (ti < n_t), si, ti

    expect = jnp.int32(0)
    for ds, dt in links:
        ok, si, ti = there(ds, dt, -1)

        @pl.when(ok)
        def _():
            pl.semaphore_signal(barrier, inc=1, device_id=dev(c, si, ti), device_id_type=MESH)

        ok, _, _ = there(ds, dt, 1)
        expect = expect + ok.astype(jnp.int32)

    first = (s * n_t + t) * shard_rows
    src_t = first // (height // 2) // frames
    src_c = first % (height // 2) // pairs
    for si in range(n_s):
        mine = (src_c == c) & (src_t == t) & (s == si)

        @pl.when(jnp.logical_not(mine))
        def _():
            pl.semaphore_signal(barrier, inc=1, device_id=dev(src_c, si, src_t), device_id_type=MESH)

    own = (src_c == c) & (src_t == t)
    expect = expect + frames * chunks * n_c - own.astype(jnp.int32)

    fold_weights(cw_ref, mw_ref, wt)
    bias = fold_bias(mw_ref, cb_ref, mb_ref)

    zero_row = jnp.zeros((frames, 1, columns, channels), BF16)

    @pl.when(c == 0)
    def _():
        xin[:, 0:1] = zero_row

    @pl.when(c == n_c - 1)
    def _():
        xin[:, half + 1 : half + 2] = zero_row

    load.wait()
    gain = gain_ref[...].reshape(1, channels)
    step_rows = 6 if (half + 2) % 6 == 0 else 2
    for f in range(frames):

        @pl.loop(0, (half + 2) // step_rows)
        def _(r):
            v = xin[f, pl.ds(r * step_rows, step_rows)].astype(F32)
            v = v.reshape(step_rows * columns, channels)
            energy = jnp.sum(v * v, axis=-1, keepdims=True) * (1.0 / channels)
            v = v * lax.rsqrt(energy + 1e-06) * gain
            v = v / (1.0 + jnp.exp(-v))
            at = pl.multiple_of(r * (step_rows * columns), step_rows * columns)
            actf[f, pl.ds(at, step_rows * columns), :] = v

    rows = half * columns
    for m in range(2):
        lo = m * (rows // 2)
        total = None
        for f in range(frames):
            for b in range(K):
                lhs = actf[f, lo + b * columns : lo + b * columns + rows // 2, :].astype(BF16)
                term = nt(lhs, wt[f * K + b])
                total = term if total is None else total + term
        acc[lo : lo + rows // 2, :] = total[:, :128]
        edge[lo : lo + rows // 2, :] = total[:, 128:]

    q = edge[...]
    w_at = lax.broadcasted_iota(jnp.int32, (rows, 128), 0) % columns
    right = jnp.where(w_at == 0, 0.0, pltpu.roll(q, 1, 0))
    left = jnp.where(w_at == columns - 1, 0.0, pltpu.roll(q, rows - 1, 0))
    acc[...] = acc[...] + right + pltpu.roll(left, 64, 1)
    rs_send[...] = edge[pl.ds(columns - 1, half, stride=columns), :].astype(BF16)
    ls_send[...] = edge[pl.ds(0, half, stride=columns), :].astype(BF16)
    quarter = rows // 4
    lane = lax.broadcasted_iota(jnp.int32, (quarter, 128), 1)
    packed = jnp.zeros((quarter, 128), F32)
    for k in range(4):
        part = pltpu.roll(acc[k * quarter : (k + 1) * quarter, :], (k * 32 + 128 - 32) % 128, 1)
        packed = jnp.where(lane // 32 == k, part, packed)
    ca_send[...] = packed.astype(BF16)

    pl.semaphore_wait(barrier, expect)

    bufs = {1: (rs_send, rs_got), -1: (ls_send, ls_got), 0: (ca_send, ca_got)}

    def link_copy(i, sign):
        ds, dt = links[i]
        ok, si, ti = there(ds, dt, sign)
        src, dst = bufs[ds]
        if ds != 0:
            dst = dst.at[dt]
        return ok, pltpu.make_async_remote_copy(
            src_ref=src, dst_ref=dst, send_sem=s1_sem.at[i], recv_sem=r1_sem.at[i],
            device_id=dev(c, si, ti), device_id_type=MESH,
        )

    for i in (2, 3, 4, 0, 1):
        ok, copy = link_copy(i, 1)

        @pl.when(ok)
        def _():
            copy.start()

    for i in (0, 1, 3, 4, 2):
        ds, dt = links[i]
        ok, copy = link_copy(i, -1)

        @pl.when(ok)
        def _():
            copy.wait_recv()
            if ds == 0:
                got = ca_got[...].astype(F32)
                for k in range(4):
                    acc[k * quarter : (k + 1) * quarter, :] += pltpu.roll(got, (128 - 32 * k) % 128, 1)
            else:
                got = bufs[ds][1][dt].astype(F32)
                turn = (128 - 32 * dt - (64 if ds < 0 else 0)) % 128
                if turn:
                    got = pltpu.roll(got, turn, 1)
                at = pl.ds(0 if ds > 0 else columns - 1, half, stride=columns)
                acc[at, :] = acc[at, :] + got

    total = acc[...] + bias
    by_row = total.reshape(pairs, 2, columns, 128)
    even = by_row[:, 0].reshape(pairs * columns, 128)
    odd = by_row[:, 1].reshape(pairs * columns, 128)
    lane = lax.broadcasted_iota(jnp.int32, (pairs * columns, 128), 1)
    mixed = jnp.where(
        lane < 16, even,
        jnp.where(
            lane < 32, pltpu.roll(odd, 16, 1),
            jnp.where(lane < 48, pltpu.roll(even, 16, 1), pltpu.roll(odd, 32, 1)),
        ),
    )
    pk[...] = mixed
    tokens = pairs * columns // 2
    left_half = pk[pl.ds(0, tokens, stride=2), :]
    right_half = pk[pl.ds(1, tokens, stride=2), :]
    lane = lax.broadcasted_iota(jnp.int32, (tokens, 128), 1)
    for f in range(frames):
        one = left_half if f == 0 else pltpu.roll(left_half, 128 - 32 * f, 1)
        two = pltpu.roll(right_half, (32 - 32 * f) % 128, 1) if f != 1 else right_half
        both = jnp.where(lane < 32, one, two)
        for m in range(chunks):
            patch[f * chunks + m] = both[m * chunk_tokens : (m + 1) * chunk_tokens, :64].astype(BF16)

    def patch_copy(f, m, ci):
        shard = ((t * frames + f) * (height // 2) + c * pairs) // shard_rows + m
        si, ti = shard // n_t, shard % n_t
        mine = (si == s) & (ti == t) & (c == ci)
        piece = f * chunks + m
        local = pltpu.make_async_copy(patch.at[piece], out_ref.at[s], r2_sem.at[s])
        away = pltpu.make_async_remote_copy(
            src_ref=patch.at[piece], dst_ref=out_ref.at[s],
            send_sem=s2_sem.at[piece * n_c + ci], recv_sem=r2_sem.at[s],
            device_id=dev(ci, si, ti), device_id_type=MESH,
        )
        return mine, local, away

    every = [(f, m, ci) for f in range(frames) for m in range(chunks) for ci in range(n_c)]
    for item in every:
        mine, local, away = patch_copy(*item)

        @pl.when(mine)
        def _():
            local.start()

        @pl.when(jnp.logical_not(mine))
        def _():
            away.start()

    for si in range(n_s):
        pltpu.make_async_copy(patch.at[0], out_ref.at[si], r2_sem.at[si]).wait()
    for i in range(5):
        ok, copy = link_copy(i, 1)

        @pl.when(ok)
        def _():
            copy.wait_send()

    for item in every:
        mine, _, away = patch_copy(*item)

        @pl.when(jnp.logical_not(mine))
        def _():
            away.wait_send()


def tail_kernel(noisy, mask, lat, pw, cw, pb, cb, shift, scale, out, comb, both, inv_ref, mean_ref, sems):
    split = lat.shape[-1]
    width = comb.shape[1]
    step = 512
    z = split // 4

    @pl.when(pl.program_id(0) == 0)
    def _():
        upper = pltpu.make_async_copy(pw, both.at[:split], sems.at[0])
        lower = pltpu.make_async_copy(cw, both.at[split:], sems.at[1])
        upper.start()
        lower.start()
        upper.wait()
        lower.wait()

    parts = comb.shape[0] // out.shape[0]

    @pl.when(pl.program_id(0) % parts == 0)
    def _():
        perm = ones_where(
            (split, split), lambda i, j: j == (i % z) * 4 + (i // z % 2) * 2 + i // (2 * z)
        ).astype(BF16)
        if len(lat.shape) == 3:
            strips, per, _ = lat.shape
            tokens = lat[...].reshape(strips * per, split)
            n, cols = strips * per, 4
            order = ones_where(
                (n, n),
                lambda i, j: j == (i // cols % strips) * per + i // (cols * strips) * cols + i % cols,
            ).astype(BF16)
            tokens = jnp.dot(order, tokens, preferred_element_type=F32).astype(BF16)
        else:
            tokens = lat[...]
        tokens = jnp.dot(tokens, perm, preferred_element_type=F32)
        own = noisy[...].astype(F32).T
        lhs = jnp.concatenate([own, tokens, mask[...].astype(F32)], axis=1).astype(BF16)
        total = None
        for k in range(0, width, step):
            at = slice(k, k + step)
            part = jnp.dot(lhs, both[:, at], preferred_element_type=F32)
            part = part + (pb[:, at] + cb[:, at])
            comb[:, at] = part
            term = jnp.sum(part, axis=-1, keepdims=True)
            total = term if total is None else total + term
        mean = total * (1.0 / width)
        square = None
        for k in range(0, width, step):
            d = comb[:, k : k + step] - mean
            term = jnp.sum(d * d, axis=-1, keepdims=True)
            square = term if square is None else square + term
        mean_ref[...] = jnp.broadcast_to(mean, mean_ref.shape)
        inv_ref[...] = jnp.broadcast_to(lax.rsqrt(square * (1.0 / width) + 1e-06), inv_ref.shape)

    rows = out.shape[0]
    mine = pl.ds(pl.multiple_of(pl.program_id(0) % parts * rows, rows), rows)
    mean, inv = mean_ref[mine, :1], inv_ref[mine, :1]
    for k in range(0, width, step):
        at = slice(k, k + step)
        out[:, at] = ((comb[mine, at] - mean) * inv * (1.0 + scale[:, at]) + shift[:, at]).astype(BF16)


def body(
    section_input, norm_gain, conv_weight, conv_bias, mean_weight, mean_bias, noisy_tokens,
    mask_tokens, patch_weight, patch_bias, context_weight, context_bias, norm_shift, norm_scale,
):
    frames, height, columns, channels = section_input.shape
    n_c, n_s, n_t = lax.axis_size("cfg"), lax.axis_size("seq"), lax.axis_size("tile")
    z = mean_weight.shape[1]
    tokens = noisy_tokens.shape[0]
    shard_rows = tokens // (n_s * columns // 2)
    half = height // n_c
    rows = half * columns
    chunks = half // 2 // shard_rows
    chunk_tokens = shard_rows * (columns // 2)
    vmem = pl.BlockSpec(memory_space=pltpu.VMEM)
    arrived = pl.pallas_call(
        functools.partial(head_kernel, (n_c, n_s, n_t, shard_rows)),
        out_shape=jax.ShapeDtypeStruct((n_s, chunk_tokens, 4 * z), BF16),
        in_specs=[pl.BlockSpec(memory_space=pltpu.HBM)] + [vmem] * 5,
        out_specs=vmem,
        scratch_shapes=[
            pltpu.VMEM((frames * K, 16 * z, channels), BF16),
            pltpu.VMEM((frames, half + 2, columns, channels), BF16),
            pltpu.VMEM((frames, (half + 2) * columns, channels), F32),
            pltpu.VMEM((rows, 128), F32),
            pltpu.VMEM((rows, 128), F32),
            pltpu.VMEM((rows // 2, 128), F32),
            pltpu.VMEM((half, 128), BF16),
            pltpu.VMEM((half, 128), BF16),
            pltpu.VMEM((rows // 4, 128), BF16),
            pltpu.VMEM((2, half, 128), BF16),
            pltpu.VMEM((2, half, 128), BF16),
            pltpu.VMEM((rows // 4, 128), BF16),
            pltpu.VMEM((frames * chunks, chunk_tokens, 4 * z), BF16),
            pltpu.SemaphoreType.DMA,
            pltpu.SemaphoreType.DMA((5,)),
            pltpu.SemaphoreType.DMA((5,)),
            pltpu.SemaphoreType.DMA((frames * chunks * n_c,)),
            pltpu.SemaphoreType.DMA((n_s,)),
        ],
        compiler_params=pltpu.CompilerParams(collective_id=0, has_side_effects=True),
        name="head",
    )(
        section_input, conv_weight.T, norm_gain, mean_weight.T, conv_bias[None], mean_bias[None]
    )
    width = patch_weight.shape[1]
    block = min(tokens, 256)
    per = block // n_s
    if per % 16 == 0 and columns == 8:
        lat = arrived
        lat_spec = pl.BlockSpec((n_s, per, 4 * z), lambda i: (0, i // parts, 0))
    else:
        lat = arrived.reshape(n_s, shard_rows, columns // 2, 4 * z).transpose(1, 0, 2, 3)
        lat = lat.reshape(tokens, 4 * z)
        lat_spec = pl.BlockSpec((block, 4 * z), lambda i: (i // parts, 0))
    parts = 2 if block % 32 == 0 else 1
    tok = lambda n: pl.BlockSpec((block, n), lambda i: (i // parts, 0))
    full = lambda a: pl.BlockSpec(a.shape, lambda i: (0, 0))
    hbm = pl.BlockSpec(memory_space=pl.ANY)
    depth = patch_weight.shape[0] + context_weight.shape[0]
    vecs = [v[None] for v in (patch_bias, context_bias, norm_shift, norm_scale)]
    return pl.pallas_call(
        tail_kernel,
        out_shape=jax.ShapeDtypeStruct((tokens, width), BF16),
        grid=(tokens // block * parts,),
        in_specs=[
            pl.BlockSpec((noisy_tokens.shape[1], block), lambda i: (0, i // parts)),
            tok(mask_tokens.shape[1]), lat_spec, hbm, hbm,
        ]
        + [full(v) for v in vecs],
        out_specs=pl.BlockSpec((block // parts, width), lambda i: (i, 0)),
        scratch_shapes=[
            pltpu.VMEM((block, width), F32),
            pltpu.VMEM((depth, width), BF16),
            pltpu.VMEM((block, 128), F32),
            pltpu.VMEM((block, 128), F32),
            pltpu.SemaphoreType.DMA((2,)),
        ],
        name="tail",
    )(noisy_tokens.T, mask_tokens, lat, patch_weight, context_weight, *vecs)


def exact_nt(x, y):
    return lax.dot_general(
        x, y, (((1,), (1,)), ((), ())), precision=lax.Precision.HIGHEST, preferred_element_type=F32
    )


def halves(v):
    high = v.astype(BF16)
    return high, (v - high.astype(F32)).astype(BF16)


def send_kernel(
    sizes, x_hbm, cw_hbm, gain_ref, mw_ref, cb_ref, mb_ref, noisy_hbm, mask_hbm, pw_hbm, xw_hbm, pb_ref, xb_ref,
    lhs_ref, both_ref, bias_ref, mean_ref, inv_ref,
    cwt, wt, xin, actf, cen, edge, msg, got, lat_w, own, mask, gram, rows, stack, lanes, in_sem, s_sem, r_sem,
):
    n_c, n_s, n_t, shard_rows = sizes
    c, s, t = lax.axis_index("cfg"), lax.axis_index("seq"), lax.axis_index("tile")
    frames, height, columns, channels = x_hbm.shape
    half = height // n_c
    pairs = half // 2
    z = mw_ref.shape[0]
    chunks = pairs // shard_rows
    reach = frames + K - 1
    split = 4 * z
    width = both_ref.shape[1]

    def dev(ci, si, ti):
        return {"cfg": ci, "seq": si, "tile": ti}

    loads = [
        pltpu.make_async_copy(
            x_hbm.at[f, pl.ds(c * (half - 1), half + 1)],
            xin.at[f, pl.ds(1 - c, half + 1)],
            in_sem.at[f],
        )
        for f in range(frames)
    ]
    for load in loads:
        load.start()
    taps = pltpu.make_async_copy(cw_hbm, cwt, in_sem.at[frames])
    taps.start()
    later = [
        pltpu.make_async_copy(noisy_hbm, own, in_sem.at[frames + 1]),
        pltpu.make_async_copy(mask_hbm, mask, in_sem.at[frames + 2]),
        pltpu.make_async_copy(xw_hbm.at[:split], lat_w, in_sem.at[frames + 3]),
        pltpu.make_async_copy(pw_hbm, both_ref.at[:split], in_sem.at[frames + 4]),
        pltpu.make_async_copy(xw_hbm.at[split:], both_ref.at[2 * split :], in_sem.at[frames + 5]),
    ]

    barrier = pltpu.get_barrier_semaphore()
    first = (s * n_t + t) * shard_rows
    frame = first // (height // 2)
    src_t = frame // frames
    src_c = first % (height // 2) // pairs
    carried = (src_t > 0) & (frame % frames < K - 1)
    for si in range(n_s):
        for back in range(2):
            mine = (src_c == c) & (src_t - back == t) & (s == si)
            wanted = jnp.logical_not(mine)
            if back:
                wanted = wanted & carried

            @pl.when(wanted)
            def _():
                pl.semaphore_signal(
                    barrier, inc=1, device_id=dev(src_c, si, src_t - back), device_id_type=MESH
                )

    def piece(g, m, ci):
        at = t * frames + g
        shard = (at * (height // 2) + c * pairs) // shard_rows + m
        si, ti = shard // n_t, shard % n_t
        mine = (si == s) & (ti == t) & (c == ci)
        valid = at < n_t * frames
        return mine, valid, si, ti

    every = [(g, m, ci) for g in range(reach) for m in range(chunks) for ci in range(n_c)]
    expect = jnp.int32(0)
    for item in every:
        mine, valid, _, _ = piece(*item)
        expect = expect + (valid & jnp.logical_not(mine)).astype(jnp.int32)

    zero_row = jnp.zeros((frames, 1, columns, channels), BF16)

    @pl.when(c == 0)
    def _():
        xin[:, 0:1] = zero_row

    @pl.when(c == n_c - 1)
    def _():
        xin[:, half + 1 : half + 2] = zero_row

    taps.wait()
    with jax.named_scope("fold"):
        fold_weights(cwt, mw_ref, wt)
        bias = fold_bias(mw_ref, cb_ref, mb_ref)

    for load in loads:
        load.wait()
    for load in later:
        load.start()
    gain = gain_ref[...].reshape(1, channels)
    step_rows = 6 if (half + 2) % 6 == 0 else 2
    with jax.named_scope("act"):
        for f in range(frames):

            @pl.loop(0, (half + 2) // step_rows)
            def _(r):
                v = xin[f, pl.ds(r * step_rows, step_rows)].astype(F32)
                v = v.reshape(step_rows * columns, channels)
                energy = jnp.sum(v * v, axis=-1, keepdims=True) * (1.0 / channels)
                v = v * lax.rsqrt(energy + 1e-06) * gain
                v = v / (1.0 + jnp.exp(-v))
                at = pl.multiple_of(r * (step_rows * columns), step_rows * columns)
                actf[f, pl.ds(at, step_rows * columns), :] = v

    count = half * columns
    with jax.named_scope("conv"):
        for m in range(2):
            lo = m * (count // 2)
            total = None
            for f in range(frames):
                for b in range(K):
                    lhs = actf[f, lo + b * columns : lo + b * columns + count // 2, :].astype(BF16)
                    term = nt(lhs, wt[f * K + b])
                    total = term if total is None else total + term
            cen[lo : lo + count // 2, :] = total[:, :128]
            edge[lo : lo + count // 2, :] = total[:, 128:]

    with jax.named_scope("pack"):
        lane = lax.broadcasted_iota(jnp.int32, (8, 128), 1)
        upper = lane >= 64
        one = lane // z % 2 == 1
        two = lane // z % 4 >= 2
        for m in range(chunks):
            cols = {}
            for a in range(2):
                mids, rights, lefts = [], [], []
                for w in range(columns):
                    starts = [((m * shard_rows + h * 8) * 2 + a) * columns + w for h in range(2)]
                    c0, c1 = (cen[pl.ds(at, 8, stride=2 * columns), :] for at in starts)
                    e0, e1 = (edge[pl.ds(at, 8, stride=2 * columns), :] for at in starts)
                    mids.append(jnp.where(upper, pltpu.roll(c1, 64, 1), c0))
                    turned = pltpu.roll(jnp.where(upper, e0, e1), 64, 1)
                    rights.append(jnp.where(upper, turned, e0))
                    lefts.append(jnp.where(upper, e1, turned))
                for w in range(columns):
                    v = mids[w]
                    if w > 0:
                        v = v + rights[w - 1]
                    if w < columns - 1:
                        v = v + lefts[w + 1]
                    cols[a, w] = v
                cols[a, columns] = rights[columns - 1]
                cols[a, columns + 1] = lefts[0]
            for j in range(columns // 2 + 1):
                p = [cols[a, 2 * j + b] for b in range(2) for a in range(2)]
                q = [None] * 4
                for k in (0, 2):
                    q[k] = jnp.where(one, pltpu.roll(p[k + 1], z, 1), p[k])
                    q[k + 1] = jnp.where(one, p[k + 1], pltpu.roll(p[k], 128 - z, 1))
                for k in range(2):
                    low = jnp.where(two, pltpu.roll(q[k + 2], 2 * z, 1), q[k])
                    high = jnp.where(two, q[k + 2], pltpu.roll(q[k], 128 - 2 * z, 1))
                    msg[k * chunks + m, j * 8 : j * 8 + 8, :] = low.astype(BF16)
                    msg[(k + 2) * chunks + m, j * 8 : j * 8 + 8, :] = high.astype(BF16)

    with jax.named_scope("barrierwait"):
        pl.semaphore_wait(barrier, expect)

    def piece_copy(g, m, ci):
        mine, valid, si, ti = piece(g, m, ci)
        slot = g // frames
        src, dst = msg.at[g * chunks + m], got.at[slot, s]
        local = pltpu.make_async_copy(src, dst, r_sem.at[slot, s])
        away = pltpu.make_async_remote_copy(
            src_ref=src, dst_ref=dst, send_sem=s_sem.at[(g * chunks + m) * n_c + ci],
            recv_sem=r_sem.at[slot, s], device_id=dev(ci, si, ti), device_id_type=MESH,
        )
        return mine & valid, jnp.logical_not(mine) & valid, local, away

    with jax.named_scope("send"):
        for item in every:
            here, there, local, away = piece_copy(*item)

            @pl.when(here)
            def _():
                local.start()

            @pl.when(there)
            def _():
                away.start()

    with jax.named_scope("prep"):
        b = pb_ref[...] + xb_ref[...]
        b = b - jnp.sum(b, axis=-1, keepdims=True) * (1.0 / width)
        bias_ref[...] = b
        for load in later:
            load.wait()
        swap = ones_where(
            (split, split), lambda i, j: j == (i % z) * 4 + (i // z % 2) * 2 + i // (2 * z)
        ).astype(BF16)
        step = 512
        for k in range(0, width, step):
            part = jnp.dot(swap, lat_w[:, k : k + step], preferred_element_type=F32)
            both_ref[split : 2 * split, k : k + step] = part.astype(BF16)
        high, rest = b.astype(BF16), None
        rest = b - high.astype(F32)
        mid = rest.astype(BF16)
        low = (rest - mid.astype(F32)).astype(BF16)
        row = lax.broadcasted_iota(jnp.int32, (8, width), 0)
        rows[...] = jnp.where(
            row == 0, 1.0,
            jnp.where(row == 1, high.astype(F32), jnp.where(row == 2, mid.astype(F32), jnp.where(row == 3, low.astype(F32), 0.0))),
        ).astype(BF16)
        energy = jnp.sum(b * b, axis=-1, keepdims=True)
        square = nt(both_ref[...], both_ref[...])
        high, low = halves(square)
        gram[0] = high
        gram[1] = low
        sums = nt(rows[...], both_ref[...])
        wmean = sums[0:1] * (1.0 / width)
        cross = (sums[1:2] + sums[2:3] + sums[3:4]) * 2.0
        noise = own[...].astype(F32).T
        lanes[...] = jnp.concatenate([noise, noise], axis=1)
        lhs_ref[:, 2 * split :] = mask[...]

    per = columns // 2 * 8
    with jax.named_scope("recv"):
        for si in range(n_s):
            pltpu.make_async_copy(msg.at[0], got.at[0, si], r_sem.at[0, si]).wait()

        @pl.when(carried)
        def _():
            for si in range(n_s):
                pltpu.make_async_copy(msg.at[0], got.at[1, si], r_sem.at[1, si]).wait()

    with jax.named_scope("assemble"):
        lane = lax.broadcasted_iota(jnp.int32, (8, 128), 1)
        odd = lane // (2 * z) % 2 == 1

        def strip(slot, si):
            v = got[slot, si, :per, :].astype(F32)
            parts = [v[k : k + 8] for k in range(0, per, 8)]
            if si > 0:
                parts[0] = parts[0] + jnp.where(odd, 0.0, got[slot, si - 1, per:, :].astype(F32))
            if si < n_s - 1:
                parts[-1] = parts[-1] + jnp.where(odd, got[slot, si + 1, per:, :].astype(F32), 0.0)
            return jnp.concatenate(parts, axis=0)

        for si in range(n_s):
            stack[si * per : (si + 1) * per, :] = strip(0, si) + bias

        @pl.when(carried)
        def _():
            for si in range(n_s):
                at = slice(si * per, (si + 1) * per)
                stack[at, :] = stack[at, :] + strip(1, si)

        n = n_s * per
        cols = columns // 2
        order = ones_where(
            (n, n), lambda i, j: j == (i // cols % n_s) * per + i % cols * 8 + i // (cols * n_s)
        ).astype(BF16)
        tokens = jnp.dot(order, stack[...].astype(BF16), preferred_element_type=F32)
        lane = lax.broadcasted_iota(jnp.int32, (n, 128), 1)
        for h in range(2):
            mine = pltpu.roll(tokens, 64, 1) if h == 0 else tokens
            at = slice(h * n, (h + 1) * n)
            lhs_ref[at, : 2 * split] = jnp.where(lane < 64, lanes[at, :], mine).astype(BF16)

    with jax.named_scope("stats"):
        block = 128
        for k in range(0, lhs_ref.shape[0], block):
            at = slice(k, k + block)
            x = lhs_ref[at, :]
            y = jnp.dot(x, gram[0], preferred_element_type=F32) + jnp.dot(x, gram[1], preferred_element_type=F32)
            x = x.astype(F32)
            mean = jnp.sum(x * wmean, axis=-1, keepdims=True)
            power = jnp.sum(x * (y + cross), axis=-1, keepdims=True) + energy
            variance = jnp.maximum(power * (1.0 / width) - mean * mean, 0.0)
            mean_ref[at, :] = jnp.broadcast_to(mean, (block, 128))
            inv_ref[at, :] = jnp.broadcast_to(lax.rsqrt(variance + 1e-06), (block, 128))

    with jax.named_scope("drain"):
        for item in every:
            _, there, _, away = piece_copy(*item)

            @pl.when(there)
            def _():
                away.wait_send()


def write_kernel(lhs, both, bias, mean, inv, shift, scale, out):
    tokens, wide = out.shape
    step = min(512, wide)
    block = 128
    for k in range(0, wide, step):
        at = slice(k, k + step)
        gain, add, move = 1.0 + scale[:, at], bias[:, at], shift[:, at]
        for r in range(0, tokens, block):
            rows = slice(r, r + block)
            part = jnp.dot(lhs[rows, :], both[:, at], preferred_element_type=F32)
            out[rows, at] = (((part + add) - mean[rows, :1]) * inv[rows, :1] * gain + move).astype(BF16)


def fast(
    section_input, norm_gain, conv_weight, conv_bias, mean_weight, mean_bias, noisy_tokens,
    mask_tokens, patch_weight, patch_bias, context_weight, context_bias, norm_shift, norm_scale,
):
    frames, height, columns, channels = section_input.shape
    n_c, n_s, n_t = lax.axis_size("cfg"), lax.axis_size("seq"), lax.axis_size("tile")
    z = mean_weight.shape[1]
    tokens, width = noisy_tokens.shape[0], patch_weight.shape[1]
    shard_rows = tokens // (n_s * columns // 2)
    half = height // n_c
    count = half * columns
    chunks = half // 2 // shard_rows
    reach = frames + K - 1
    per = (columns // 2 + 1) * 8
    depth = patch_weight.shape[0] + context_weight.shape[0]
    split = 4 * z
    vmem = pl.BlockSpec(memory_space=pltpu.VMEM)
    hbm = pl.BlockSpec(memory_space=pltpu.HBM)
    n = n_s * columns // 2 * 8
    prepared = pl.pallas_call(
        functools.partial(send_kernel, (n_c, n_s, n_t, shard_rows)),
        out_shape=(
            pltpu.VMEM((tokens, depth), BF16),
            pltpu.VMEM((depth, width), BF16),
            pltpu.VMEM((1, width), F32),
            pltpu.VMEM((tokens, 128), F32),
            pltpu.VMEM((tokens, 128), F32),
        ),
        in_specs=[hbm, hbm] + [vmem] * 4 + [hbm] * 4 + [vmem] * 2,
        out_specs=(vmem,) * 5,
        scratch_shapes=[
            pltpu.VMEM(conv_weight.shape[::-1], BF16),
            pltpu.VMEM((frames * K, 16 * z, channels), BF16),
            pltpu.VMEM((frames, half + 2, columns, channels), BF16),
            pltpu.VMEM((frames, (half + 2) * columns, channels), F32),
            pltpu.VMEM((count, 128), F32),
            pltpu.VMEM((count, 128), F32),
            pltpu.VMEM((reach * chunks, per, 128), BF16),
            pltpu.VMEM((2, n_s, per, 128), BF16),
            pltpu.VMEM((split, width), BF16),
            pltpu.VMEM(noisy_tokens.shape[::-1], BF16),
            pltpu.VMEM(mask_tokens.shape, BF16),
            pltpu.VMEM((2, depth, depth), BF16),
            pltpu.VMEM((8, width), BF16),
            pltpu.VMEM((n, 128), F32),
            pltpu.VMEM((tokens, 128), F32),
            pltpu.SemaphoreType.DMA((frames + 6,)),
            pltpu.SemaphoreType.DMA((reach * chunks * n_c,)),
            pltpu.SemaphoreType.DMA((2, n_s)),
        ],
        compiler_params=pltpu.CompilerParams(
            collective_id=0, has_side_effects=True, vmem_limit_bytes=40 * 2**20
        ),
        name="send",
    )(
        *(
            pltpu.with_memory_space_constraint(v, pltpu.HBM)
            for v in (
                section_input, conv_weight.T, norm_gain, mean_weight.T, conv_bias[None], mean_bias[None],
                noisy_tokens.T, mask_tokens, patch_weight, context_weight, patch_bias[None], context_bias[None],
            )
        )
    )
    wide = width // 5 if width % (5 * 512) == 0 else width
    col = lambda r: pl.BlockSpec((r, wide), lambda i: (0, i))
    full = lambda a: pl.BlockSpec(a.shape, lambda i: (0, 0))
    lhs, both, bias, mean, inv = prepared
    return pl.pallas_call(
        write_kernel,
        out_shape=jax.ShapeDtypeStruct((tokens, width), BF16),
        grid=(width // wide,),
        in_specs=[full(lhs), col(depth), col(1), full(mean), full(inv), col(1), col(1)],
        out_specs=col(tokens),
        compiler_params=pltpu.CompilerParams(vmem_limit_bytes=24 * 2**20),
        name="write",
    )(*prepared, norm_shift[None], norm_scale[None])


def choose(*args):
    n_c, n_s, n_t = lax.axis_size("cfg"), lax.axis_size("seq"), lax.axis_size("tile")
    frames, height, columns, _ = args[0].shape
    rows = args[6].shape[0] // (n_s * columns // 2)
    fits = columns == 8 and args[4].shape[1] == 16 and frames == 2 and rows == 16
    fits = fits and height // n_c // 2 % rows == 0
    return fast(*args) if fits else body(*args)


def solution(mesh):
    placed = (P("tile", None, "seq", None),) + (P(),) * 5
    placed = placed + (P(("seq", "tile"), None),) * 2 + (P(),) * 6
    return jax.shard_map(
        choose, mesh=mesh, in_specs=placed, out_specs=P(("seq", "tile"), None), check_vma=False
    )
```

```python
import functools

import jax
import jax.numpy as jnp
from jax import lax
from jax.experimental import pallas as pl
from jax.experimental.pallas import tpu as pltpu
from jax.sharding import PartitionSpec as P

K = 3
MESH = pl.DeviceIdType.MESH
F32 = jnp.float32
BF16 = jnp.bfloat16


def ones_where(shape, test):
    i = lax.broadcasted_iota(jnp.int32, shape, 0)
    j = lax.broadcasted_iota(jnp.int32, shape, 1)
    return jnp.where(test(i, j), 1.0, 0.0)


def nt(x, y):
    return lax.dot_general(x, y, (((1,), (1,)), ((), ())), preferred_element_type=F32)


def fold_weights(cw_ref, mw_ref, wt):
    z, zo = mw_ref.shape
    mw = mw_ref[...]
    high = mw.astype(BF16)
    low = (mw - high.astype(F32)).astype(BF16)
    spread = ones_where((4 * z, z), lambda i, j: i % z == j).astype(BF16)
    copier = ones_where((zo, K * zo), lambda i, j: j % zo == i).astype(BF16)

    def right_slot(i, j):
        slot, e = i // z, j // zo
        return ((slot == 0) & (e == 1)) | ((slot == 2) & (e == 0)) | ((slot == 3) & (e == 2))

    keep = ones_where((4 * z, K * zo), right_slot)
    parts = []
    for part in (high, low):
        tall = jnp.dot(spread, part, preferred_element_type=F32).astype(BF16)
        parts.append((jnp.dot(tall, copier, preferred_element_type=F32) * keep).astype(BF16))
    parts = jnp.concatenate(parts, axis=0)
    nothing = jnp.zeros((z, wt.shape[2]), BF16)
    for a in range(K):
        for b in range(K):
            at = (a * K + b) * K * zo
            rhs = cw_ref[at : at + K * zo, :]
            res = jnp.dot(parts, rhs, preferred_element_type=F32)
            res = (res[: 4 * z] + res[4 * z :]).astype(BF16)
            for f in range(2):
                for slot in range(4):
                    row = slot * 4 * z + (f + 2 - a) * z
                    wt[f * K + b, row : row + z, :] = res[slot * z : (slot + 1) * z]
    for b in range(K):
        for slot in range(4):
            row = slot * 4 * z
            wt[b, row + 3 * z : row + 4 * z, :] = nothing
            wt[K + b, row : row + z, :] = nothing


def fold_bias(mw_ref, cb_ref, mb_ref):
    z = mw_ref.shape[0]
    copier = ones_where((128, z), lambda i, j: i % z == j)
    exact = functools.partial(
        lax.dot_general, dimension_numbers=(((1,), (1,)), ((), ())),
        precision=lax.Precision.HIGHEST, preferred_element_type=F32,
    )
    return exact(exact(cb_ref[...], mw_ref[...]) + mb_ref[...], copier)


def head_kernel(
    sizes, x_hbm, cw_ref, gain_ref, mw_ref, cb_ref, mb_ref, out_ref,
    wt, xin, actf, acc, edge, pk, rs_send, ls_send, ca_send, rs_got, ls_got, ca_got, patch,
    in_sem, s1_sem, r1_sem, s2_sem, r2_sem,
):
    n_c, n_s, n_t, shard_rows = sizes
    c, s, t = lax.axis_index("cfg"), lax.axis_index("seq"), lax.axis_index("tile")
    frames, height, columns, channels = x_hbm.shape
    half = height // n_c
    pairs = half // 2
    z = 16
    chunks = pairs // shard_rows
    chunk_tokens = shard_rows * (columns // 2)

    def dev(ci, si, ti):
        return {"cfg": ci, "seq": si, "tile": ti}

    load = pltpu.make_async_copy(
        x_hbm.at[:, pl.ds(c * (half - 1), half + 1)],
        xin.at[:, pl.ds(1 - c, half + 1)],
        in_sem,
    )
    load.start()

    barrier = pltpu.get_barrier_semaphore()
    links = [(1, 0), (-1, 0), (0, 1), (1, 1), (-1, 1)]

    def there(ds, dt, sign):
        si, ti = s + sign * ds, t + sign * dt
        return (si >= 0) & (si < n_s) & (ti >= 0) & (ti < n_t), si, ti

    expect = jnp.int32(0)
    for ds, dt in links:
        ok, si, ti = there(ds, dt, -1)

        @pl.when(ok)
        def _():
            pl.semaphore_signal(barrier, inc=1, device_id=dev(c, si, ti), device_id_type=MESH)

        ok, _, _ = there(ds, dt, 1)
        expect = expect + ok.astype(jnp.int32)

    first = (s * n_t + t) * shard_rows
    src_t = first // (height // 2) // frames
    src_c = first % (height // 2) // pairs
    for si in range(n_s):
        mine = (src_c == c) & (src_t == t) & (s == si)

        @pl.when(jnp.logical_not(mine))
        def _():
            pl.semaphore_signal(barrier, inc=1, device_id=dev(src_c, si, src_t), device_id_type=MESH)

    own = (src_c == c) & (src_t == t)
    expect = expect + frames * chunks * n_c - own.astype(jnp.int32)

    fold_weights(cw_ref, mw_ref, wt)
    bias = fold_bias(mw_ref, cb_ref, mb_ref)

    zero_row = jnp.zeros((frames, 1, columns, channels), BF16)

    @pl.when(c == 0)
    def _():
        xin[:, 0:1] = zero_row

    @pl.when(c == n_c - 1)
    def _():
        xin[:, half + 1 : half + 2] = zero_row

    load.wait()
    gain = gain_ref[...].reshape(1, channels)
    step_rows = 6 if (half + 2) % 6 == 0 else 2
    for f in range(frames):

        @pl.loop(0, (half + 2) // step_rows)
        def _(r):
            v = xin[f, pl.ds(r * step_rows, step_rows)].astype(F32)
            v = v.reshape(step_rows * columns, channels)
            energy = jnp.sum(v * v, axis=-1, keepdims=True) * (1.0 / channels)
            v = v * lax.rsqrt(energy + 1e-06) * gain
            v = v / (1.0 + jnp.exp(-v))
            at = pl.multiple_of(r * (step_rows * columns), step_rows * columns)
            actf[f, pl.ds(at, step_rows * columns), :] = v

    rows = half * columns
    for m in range(2):
        lo = m * (rows // 2)
        total = None
        for f in range(frames):
            for b in range(K):
                lhs = actf[f, lo + b * columns : lo + b * columns + rows // 2, :].astype(BF16)
                term = nt(lhs, wt[f * K + b])
                total = term if total is None else total + term
        acc[lo : lo + rows // 2, :] = total[:, :128]
        edge[lo : lo + rows // 2, :] = total[:, 128:]

    q = edge[...]
    w_at = lax.broadcasted_iota(jnp.int32, (rows, 128), 0) % columns
    right = jnp.where(w_at == 0, 0.0, pltpu.roll(q, 1, 0))
    left = jnp.where(w_at == columns - 1, 0.0, pltpu.roll(q, rows - 1, 0))
    acc[...] = acc[...] + right + pltpu.roll(left, 64, 1)
    rs_send[...] = edge[pl.ds(columns - 1, half, stride=columns), :].astype(BF16)
    ls_send[...] = edge[pl.ds(0, half, stride=columns), :].astype(BF16)
    quarter = rows // 4
    lane = lax.broadcasted_iota(jnp.int32, (quarter, 128), 1)
    packed = jnp.zeros((quarter, 128), F32)
    for k in range(4):
        part = pltpu.roll(acc[k * quarter : (k + 1) * quarter, :], (k * 32 + 128 - 32) % 128, 1)
        packed = jnp.where(lane // 32 == k, part, packed)
    ca_send[...] = packed.astype(BF16)

    pl.semaphore_wait(barrier, expect)

    bufs = {1: (rs_send, rs_got), -1: (ls_send, ls_got), 0: (ca_send, ca_got)}

    def link_copy(i, sign):
        ds, dt = links[i]
        ok, si, ti = there(ds, dt, sign)
        src, dst = bufs[ds]
        if ds != 0:
            dst = dst.at[dt]
        return ok, pltpu.make_async_remote_copy(
            src_ref=src, dst_ref=dst, send_sem=s1_sem.at[i], recv_sem=r1_sem.at[i],
            device_id=dev(c, si, ti), device_id_type=MESH,
        )

    for i in (2, 3, 4, 0, 1):
        ok, copy = link_copy(i, 1)

        @pl.when(ok)
        def _():
            copy.start()

    for i in (0, 1, 3, 4, 2):
        ds, dt = links[i]
        ok, copy = link_copy(i, -1)

        @pl.when(ok)
        def _():
            copy.wait_recv()
            if ds == 0:
                got = ca_got[...].astype(F32)
                for k in range(4):
                    acc[k * quarter : (k + 1) * quarter, :] += pltpu.roll(got, (128 - 32 * k) % 128, 1)
            else:
                got = bufs[ds][1][dt].astype(F32)
                turn = (128 - 32 * dt - (64 if ds < 0 else 0)) % 128
                if turn:
                    got = pltpu.roll(got, turn, 1)
                at = pl.ds(0 if ds > 0 else columns - 1, half, stride=columns)
                acc[at, :] = acc[at, :] + got

    total = acc[...] + bias
    by_row = total.reshape(pairs, 2, columns, 128)
    even = by_row[:, 0].reshape(pairs * columns, 128)
    odd = by_row[:, 1].reshape(pairs * columns, 128)
    lane = lax.broadcasted_iota(jnp.int32, (pairs * columns, 128), 1)
    mixed = jnp.where(
        lane < 16, even,
        jnp.where(
            lane < 32, pltpu.roll(odd, 16, 1),
            jnp.where(lane < 48, pltpu.roll(even, 16, 1), pltpu.roll(odd, 32, 1)),
        ),
    )
    pk[...] = mixed
    tokens = pairs * columns // 2
    left_half = pk[pl.ds(0, tokens, stride=2), :]
    right_half = pk[pl.ds(1, tokens, stride=2), :]
    lane = lax.broadcasted_iota(jnp.int32, (tokens, 128), 1)
    for f in range(frames):
        one = left_half if f == 0 else pltpu.roll(left_half, 128 - 32 * f, 1)
        two = pltpu.roll(right_half, (32 - 32 * f) % 128, 1) if f != 1 else right_half
        both = jnp.where(lane < 32, one, two)
        for m in range(chunks):
            patch[f * chunks + m] = both[m * chunk_tokens : (m + 1) * chunk_tokens, :64].astype(BF16)

    def patch_copy(f, m, ci):
        shard = ((t * frames + f) * (height // 2) + c * pairs) // shard_rows + m
        si, ti = shard // n_t, shard % n_t
        mine = (si == s) & (ti == t) & (c == ci)
        piece = f * chunks + m
        local = pltpu.make_async_copy(patch.at[piece], out_ref.at[s], r2_sem.at[s])
        away = pltpu.make_async_remote_copy(
            src_ref=patch.at[piece], dst_ref=out_ref.at[s],
            send_sem=s2_sem.at[piece * n_c + ci], recv_sem=r2_sem.at[s],
            device_id=dev(ci, si, ti), device_id_type=MESH,
        )
        return mine, local, away

    every = [(f, m, ci) for f in range(frames) for m in range(chunks) for ci in range(n_c)]
    for item in every:
        mine, local, away = patch_copy(*item)

        @pl.when(mine)
        def _():
            local.start()

        @pl.when(jnp.logical_not(mine))
        def _():
            away.start()

    for si in range(n_s):
        pltpu.make_async_copy(patch.at[0], out_ref.at[si], r2_sem.at[si]).wait()
    for i in range(5):
        ok, copy = link_copy(i, 1)

        @pl.when(ok)
        def _():
            copy.wait_send()

    for item in every:
        mine, _, away = patch_copy(*item)

        @pl.when(jnp.logical_not(mine))
        def _():
            away.wait_send()


def tail_kernel(noisy, mask, lat, pw, cw, pb, cb, shift, scale, out, comb, both, inv_ref, mean_ref, sems):
    split = lat.shape[-1]
    width = comb.shape[1]
    step = 512
    z = split // 4

    @pl.when(pl.program_id(0) == 0)
    def _():
        upper = pltpu.make_async_copy(pw, both.at[:split], sems.at[0])
        lower = pltpu.make_async_copy(cw, both.at[split:], sems.at[1])
        upper.start()
        lower.start()
        upper.wait()
        lower.wait()

    parts = comb.shape[0] // out.shape[0]

    @pl.when(pl.program_id(0) % parts == 0)
    def _():
        perm = ones_where(
            (split, split), lambda i, j: j == (i % z) * 4 + (i // z % 2) * 2 + i // (2 * z)
        ).astype(BF16)
        if len(lat.shape) == 3:
            strips, per, _ = lat.shape
            tokens = lat[...].reshape(strips * per, split)
            n, cols = strips * per, 4
            order = ones_where(
                (n, n),
                lambda i, j: j == (i // cols % strips) * per + i // (cols * strips) * cols + i % cols,
            ).astype(BF16)
            tokens = jnp.dot(order, tokens, preferred_element_type=F32).astype(BF16)
        else:
            tokens = lat[...]
        tokens = jnp.dot(tokens, perm, preferred_element_type=F32)
        own = noisy[...].astype(F32).T
        lhs = jnp.concatenate([own, tokens, mask[...].astype(F32)], axis=1).astype(BF16)
        total = None
        for k in range(0, width, step):
            at = slice(k, k + step)
            part = jnp.dot(lhs, both[:, at], preferred_element_type=F32)
            part = part + (pb[:, at] + cb[:, at])
            comb[:, at] = part
            term = jnp.sum(part, axis=-1, keepdims=True)
            total = term if total is None else total + term
        mean = total * (1.0 / width)
        square = None
        for k in range(0, width, step):
            d = comb[:, k : k + step] - mean
            term = jnp.sum(d * d, axis=-1, keepdims=True)
            square = term if square is None else square + term
        mean_ref[...] = jnp.broadcast_to(mean, mean_ref.shape)
        inv_ref[...] = jnp.broadcast_to(lax.rsqrt(square * (1.0 / width) + 1e-06), inv_ref.shape)

    rows = out.shape[0]
    mine = pl.ds(pl.multiple_of(pl.program_id(0) % parts * rows, rows), rows)
    mean, inv = mean_ref[mine, :1], inv_ref[mine, :1]
    for k in range(0, width, step):
        at = slice(k, k + step)
        out[:, at] = ((comb[mine, at] - mean) * inv * (1.0 + scale[:, at]) + shift[:, at]).astype(BF16)


def body(
    section_input, norm_gain, conv_weight, conv_bias, mean_weight, mean_bias, noisy_tokens,
    mask_tokens, patch_weight, patch_bias, context_weight, context_bias, norm_shift, norm_scale,
):
    frames, height, columns, channels = section_input.shape
    n_c, n_s, n_t = lax.axis_size("cfg"), lax.axis_size("seq"), lax.axis_size("tile")
    z = mean_weight.shape[1]
    tokens = noisy_tokens.shape[0]
    shard_rows = tokens // (n_s * columns // 2)
    half = height // n_c
    rows = half * columns
    chunks = half // 2 // shard_rows
    chunk_tokens = shard_rows * (columns // 2)
    vmem = pl.BlockSpec(memory_space=pltpu.VMEM)
    arrived = pl.pallas_call(
        functools.partial(head_kernel, (n_c, n_s, n_t, shard_rows)),
        out_shape=jax.ShapeDtypeStruct((n_s, chunk_tokens, 4 * z), BF16),
        in_specs=[pl.BlockSpec(memory_space=pltpu.HBM)] + [vmem] * 5,
        out_specs=vmem,
        scratch_shapes=[
            pltpu.VMEM((frames * K, 16 * z, channels), BF16),
            pltpu.VMEM((frames, half + 2, columns, channels), BF16),
            pltpu.VMEM((frames, (half + 2) * columns, channels), F32),
            pltpu.VMEM((rows, 128), F32),
            pltpu.VMEM((rows, 128), F32),
            pltpu.VMEM((rows // 2, 128), F32),
            pltpu.VMEM((half, 128), BF16),
            pltpu.VMEM((half, 128), BF16),
            pltpu.VMEM((rows // 4, 128), BF16),
            pltpu.VMEM((2, half, 128), BF16),
            pltpu.VMEM((2, half, 128), BF16),
            pltpu.VMEM((rows // 4, 128), BF16),
            pltpu.VMEM((frames * chunks, chunk_tokens, 4 * z), BF16),
            pltpu.SemaphoreType.DMA,
            pltpu.SemaphoreType.DMA((5,)),
            pltpu.SemaphoreType.DMA((5,)),
            pltpu.SemaphoreType.DMA((frames * chunks * n_c,)),
            pltpu.SemaphoreType.DMA((n_s,)),
        ],
        compiler_params=pltpu.CompilerParams(collective_id=0, has_side_effects=True),
        name="head",
    )(
        section_input, conv_weight.T, norm_gain, mean_weight.T, conv_bias[None], mean_bias[None]
    )
    width = patch_weight.shape[1]
    block = min(tokens, 256)
    per = block // n_s
    if per % 16 == 0 and columns == 8:
        lat = arrived
        lat_spec = pl.BlockSpec((n_s, per, 4 * z), lambda i: (0, i // parts, 0))
    else:
        lat = arrived.reshape(n_s, shard_rows, columns // 2, 4 * z).transpose(1, 0, 2, 3)
        lat = lat.reshape(tokens, 4 * z)
        lat_spec = pl.BlockSpec((block, 4 * z), lambda i: (i // parts, 0))
    parts = 2 if block % 32 == 0 else 1
    tok = lambda n: pl.BlockSpec((block, n), lambda i: (i // parts, 0))
    full = lambda a: pl.BlockSpec(a.shape, lambda i: (0, 0))
    hbm = pl.BlockSpec(memory_space=pl.ANY)
    depth = patch_weight.shape[0] + context_weight.shape[0]
    vecs = [v[None] for v in (patch_bias, context_bias, norm_shift, norm_scale)]
    return pl.pallas_call(
        tail_kernel,
        out_shape=jax.ShapeDtypeStruct((tokens, width), BF16),
        grid=(tokens // block * parts,),
        in_specs=[
            pl.BlockSpec((noisy_tokens.shape[1], block), lambda i: (0, i // parts)),
            tok(mask_tokens.shape[1]), lat_spec, hbm, hbm,
        ]
        + [full(v) for v in vecs],
        out_specs=pl.BlockSpec((block // parts, width), lambda i: (i, 0)),
        scratch_shapes=[
            pltpu.VMEM((block, width), F32),
            pltpu.VMEM((depth, width), BF16),
            pltpu.VMEM((block, 128), F32),
            pltpu.VMEM((block, 128), F32),
            pltpu.SemaphoreType.DMA((2,)),
        ],
        name="tail",
    )(noisy_tokens.T, mask_tokens, lat, patch_weight, context_weight, *vecs)


def fold_taps(cw_ref, mw_ref, wt):
    z, zo = mw_ref.shape
    channels = cw_ref.shape[1]
    mw = mw_ref[...]
    high = mw.astype(BF16)
    low = (mw - high.astype(F32)).astype(BF16)
    spread = ones_where((4 * z, z), lambda i, j: i % z == j).astype(BF16)
    copier = ones_where((zo, K * zo), lambda i, j: j % zo == i).astype(BF16)

    def right_slot(i, j):
        slot, e = i // z, j // zo
        return ((slot == 0) & (e == 1)) | ((slot == 2) & (e == 0)) | ((slot == 3) & (e == 2))

    keep = ones_where((4 * z, K * zo), right_slot)
    parts = []
    for part in (high, low):
        tall = jnp.dot(spread, part, preferred_element_type=F32).astype(BF16)
        parts.append((jnp.dot(tall, copier, preferred_element_type=F32) * keep).astype(BF16))
    nothing = jnp.zeros((z, channels), BF16)
    for a in range(K):
        for b in range(K):
            at = (a * K + b) * K * zo
            tap = cw_ref[at : at + K * zo, :]
            res = jnp.dot(parts[0], tap, preferred_element_type=F32)
            res = res + jnp.dot(parts[1], tap, preferred_element_type=F32)
            res = res.astype(BF16)
            for f in range(2):
                for slot in range(4):
                    row = slot * 4 * z + (f + 2 - a) * z
                    wt[row : row + z, (f * K + b) * channels : (f * K + b + 1) * channels] = res[
                        slot * z : (slot + 1) * z
                    ]
    for b in range(K):
        for slot in range(4):
            row = slot * 4 * z
            wt[row + 3 * z : row + 4 * z, b * channels : (b + 1) * channels] = nothing
            wt[row : row + z, (K + b) * channels : (K + b + 1) * channels] = nothing


def halves(v):
    high = v.astype(BF16)
    return high, (v - high.astype(F32)).astype(BF16)


def send_kernel(
    sizes, x_hbm, cw_hbm, gain_hbm, mw_hbm, cb_hbm, mb_hbm, noisy_hbm, mask_hbm, pw_hbm, xw_hbm, pb_hbm,
    xb_hbm, scale_hbm, lhs_ref, late_ref, early_ref, inv_ref,
    cwt, gain_ref, mw_ref, cb_ref, mb_ref, pb_ref, xb_ref, scale_ref, wt, xin, actf, cen, edge, stack, msg, got,
    lat_w, both, own, gram, own_gram, order, swap, bias_row, center, late_mean, x_early, base, in_sem, s_sem, r_sem,
):
    n_c, n_s, n_t, shard_rows = sizes
    c, s, t = lax.axis_index("cfg"), lax.axis_index("seq"), lax.axis_index("tile")
    frames, height, columns, channels = x_hbm.shape
    half = height // n_c
    pairs = half // 2
    z = mw_ref.shape[0]
    chunks = pairs // shard_rows
    reach = frames + K - 1
    split = 4 * z
    width = late_ref.shape[1]
    tokens = lhs_ref.shape[0]
    depth = pw_hbm.shape[0] + xw_hbm.shape[0]

    def dev(ci, si, ti):
        return {"cfg": ci, "seq": si, "tile": ti}

    cut = half // 2 + 2
    start = c * (half - 1)
    xs = [
        pltpu.make_async_copy(
            x_hbm.at[:, pl.ds(start + lo, size)], xin.at[:, pl.ds(1 - c + lo, size)], in_sem.at[i]
        )
        for i, (lo, size) in enumerate(((0, cut), (cut, half + 1 - cut)))
    ]
    small = [
        pltpu.make_async_copy(src, dst, in_sem.at[2 + i])
        for i, (src, dst) in enumerate(
            ((gain_hbm, gain_ref), (mw_hbm, mw_ref), (cb_hbm, cb_ref), (mb_hbm, mb_ref), (cw_hbm, cwt))
        )
    ]
    later = [
        pltpu.make_async_copy(src, dst, in_sem.at[7 + i])
        for i, (src, dst) in enumerate(
            (
                (pb_hbm, pb_ref), (xb_hbm, xb_ref), (scale_hbm, scale_ref), (noisy_hbm, own),
                (mask_hbm, x_early.at[:, 2 * split :]), (xw_hbm.at[:split], lat_w),
                (pw_hbm, both.at[:split]), (xw_hbm.at[split:], both.at[2 * split : depth]),
            )
        )
    ]
    xs[0].start()
    for load in small:
        load.start()
    xs[1].start()

    barrier = pltpu.get_barrier_semaphore()
    first = (s * n_t + t) * shard_rows
    frame = first // (height // 2)
    src_t = frame // frames
    src_c = first % (height // 2) // pairs
    carried = (src_t > 0) & (frame % frames < K - 1)
    for si in range(n_s):
        for back in range(2):
            mine = (src_c == c) & (src_t - back == t) & (s == si)
            wanted = jnp.logical_not(mine)
            if back:
                wanted = wanted & carried

            @pl.when(wanted)
            def _():
                pl.semaphore_signal(
                    barrier, inc=1, device_id=dev(src_c, si, src_t - back), device_id_type=MESH
                )

    def place(g, m):
        shard = ((t * frames + g) * (height // 2) + c * pairs) // shard_rows + m
        return shard // n_t, shard % n_t

    own_main = (src_c == c) & (src_t == t)
    own_carry = (src_c == c) & (src_t - 1 == t) & carried
    more = t + 1 < n_t
    expect = frames * chunks * n_c - own_main.astype(jnp.int32)
    rest = (reach - frames) * chunks * n_c - own_carry.astype(jnp.int32)
    expect = expect + jnp.where(more, rest, 0)

    zero_row = jnp.zeros((frames, 1, columns, channels), BF16)

    @pl.when(c == 0)
    def _():
        xin[:, 0:1] = zero_row

    @pl.when(c == n_c - 1)
    def _():
        xin[:, half + 1 : half + 2] = zero_row

    def activate(lo, hi):
        step = 2
        for f in range(frames):
            for r in range(lo, hi, step):
                v = xin[f, r : r + step].astype(F32).reshape(step * columns, channels)
                energy = jnp.sum(v * v, axis=-1, keepdims=True) * (1.0 / channels)
                v = v * lax.rsqrt(energy + 1e-06) * gain
                actf[f, r * columns : (r + step) * columns, :] = v + v * jnp.tanh(v)

    count = half * columns // 2

    def convolve(m):
        lo = m * count
        for f in range(frames):
            taps = [actf[f, lo + b * columns : lo + b * columns + count, :].astype(BF16) for b in range(K)]
            total = nt(jnp.concatenate(taps, axis=1), wt[:, f * K * channels : (f + 1) * K * channels])
            cen[f, lo : lo + count, :] = total[:, :128]
            edge[f, lo : lo + count, :] = total[:, 128:]

    def both_frames(ref, at):
        v = ref[0, pl.ds(at, 8, stride=2 * columns), :]
        for f in range(1, frames):
            v = v + ref[f, pl.ds(at, 8, stride=2 * columns), :]
        return v

    lane = lax.broadcasted_iota(jnp.int32, (8, 128), 1)
    upper = lane >= 64
    one = lane // z % 2 == 1
    two = lane // z % 4 >= 2

    def pack(m):
        cols = {}
        for a in range(2):
            mids, rights, lefts = [], [], []
            for w in range(columns):
                starts = [((m * shard_rows + h * 8) * 2 + a) * columns + w for h in range(2)]
                c0, c1 = (both_frames(cen, at) for at in starts)
                e0, e1 = (both_frames(edge, at) for at in starts)
                mids.append(jnp.where(upper, pltpu.roll(c1, 64, 1), c0))
                turned = pltpu.roll(jnp.where(upper, e0, e1), 64, 1)
                rights.append(jnp.where(upper, turned, e0))
                lefts.append(jnp.where(upper, e1, turned))
            for w in range(columns):
                v = mids[w]
                if w > 0:
                    v = v + rights[w - 1]
                if w < columns - 1:
                    v = v + lefts[w + 1]
                cols[a, w] = v
            cols[a, columns] = rights[columns - 1]
            cols[a, columns + 1] = lefts[0]
        for j in range(columns // 2 + 1):
            p = [cols[a, 2 * j + b] for b in range(2) for a in range(2)]
            q = [None] * 4
            for k in (0, 2):
                q[k] = jnp.where(one, pltpu.roll(p[k + 1], z, 1), p[k])
                q[k + 1] = jnp.where(one, p[k + 1], pltpu.roll(p[k], 128 - z, 1))
            for k in range(2):
                low = jnp.where(two, pltpu.roll(q[k + 2], 2 * z, 1), q[k])
                high = jnp.where(two, q[k + 2], pltpu.roll(q[k], 128 - 2 * z, 1))
                msg[k * chunks + m, j * 8 : j * 8 + 8, :] = low.astype(BF16)
                msg[(k + 2) * chunks + m, j * 8 : j * 8 + 8, :] = high.astype(BF16)

    def send(m):
        def post(g):
            si, ti = place(g, m)
            here = (si == s) & (ti == t)
            slot = g // frames
            src, dst = msg.at[g * chunks + m], got.at[slot, s]
            for ci in range(n_c):

                @pl.when(here & (c == ci))
                def _():
                    pltpu.make_async_copy(src, dst, r_sem.at[slot]).start()

                @pl.when(jnp.logical_not(here & (c == ci)))
                def _():
                    pltpu.make_async_remote_copy(
                        src_ref=src, dst_ref=dst, send_sem=s_sem.at[slot, ci], recv_sem=r_sem.at[slot],
                        device_id=dev(ci, si, ti), device_id_type=MESH,
                    ).start()

        for g in range(frames):
            post(g)

        @pl.when(more)
        def _():
            for g in range(frames, reach):
                post(g)

    per = columns // 2 * 8
    n = n_s * per
    cols = columns // 2
    with jax.named_scope("tables"):
        i = lax.broadcasted_iota(jnp.int32, (n, n), 0)
        j = lax.broadcasted_iota(jnp.int32, (n, n), 1)
        wanted = ((i & (cols * n_s - 1)) // cols) * per + (i & (cols - 1)) * 8 + i // (cols * n_s)
        order[...] = jnp.where(j == wanted, 1.0, 0.0).astype(BF16)
        i = lax.broadcasted_iota(jnp.int32, (split, split), 0)
        j = lax.broadcasted_iota(jnp.int32, (split, split), 1)
        swap[...] = jnp.where(j == (i & (z - 1)) * 4 + (i // z & 1) * 2 + i // (2 * z), 1.0, 0.0).astype(BF16)
    with jax.named_scope("load0"):
        for load in small[:4]:
            load.wait()
    with jax.named_scope("loadx"):
        xs[0].wait()
    with jax.named_scope("loadt"):
        small[4].wait()
        for load in later:
            load.start()
    with jax.named_scope("fold"):
        gain = gain_ref[...].reshape(1, channels) * 0.5
        fold_taps(cwt, mw_ref, wt)
        activate(0, half // 2 + 2)
    with jax.named_scope("load1"):
        xs[1].wait()
    with jax.named_scope("conv0"):
        convolve(0)
        activate(half // 2 + 2, half + 2)
        pack(0)
    ahead = ((s == 0) & (t == 0)).astype(jnp.int32)
    block = 128

    @pl.loop(0, 2)
    def _(turn):
        @pl.when(turn == ahead)
        def _():
            with jax.named_scope("barrierwait"):
                pl.semaphore_wait(barrier, expect)
            with jax.named_scope("send0"):
                send(0)

        @pl.when(turn == 0)
        def _():
            with jax.named_scope("conv1"):
                convolve(1)
                pack(1)

        @pl.when(turn == ahead)
        def _():
            with jax.named_scope("send1"):
                send(1)

        @pl.when(turn == 1 - ahead)
        def _():
            with jax.named_scope("loadw"):
                for load in later:
                    load.wait()
            with jax.named_scope("prep"):
                bias_row[...] = fold_bias(mw_ref, cb_ref, mb_ref)
                b = pb_ref[...] + xb_ref[...]
                b = b - jnp.sum(b, axis=-1, keepdims=True) * (1.0 / width)
                scaled = scale_ref[...] + 1.0
                center[0] = b
                center[1] = scaled
                step = 512
                row = lax.broadcasted_iota(jnp.int32, (16, step), 0)
                for k in range(0, width, step):
                    at = slice(k, k + step)
                    part = jnp.dot(swap[...], lat_w[:, at], preferred_element_type=F32)
                    both[split : 2 * split, at] = part.astype(BF16)
                    high, low = halves(part * scaled[:, at])
                    late_ref[:split, at] = high
                    late_ref[split : 2 * split, at] = low
                    high = scaled[:, at].astype(BF16).astype(F32)
                    low = scaled[:, at] - high
                    four = jnp.where(row % 2 == 0, high, low)
                    late_ref[2 * split :, at] = jnp.where(row < 4, four, 0.0).astype(BF16)
                high = b.astype(BF16).astype(F32)
                mid = (b - high).astype(BF16).astype(F32)
                row = lax.broadcasted_iota(jnp.int32, (16, width), 0)
                picked = jnp.where(row == 0, 1.0, jnp.where(row == 1, high, jnp.where(row == 2, mid, b - high - mid)))
                both[depth:, :] = jnp.where(row < 4, picked, 0.0).astype(BF16)
                noise = own[...].astype(F32).T
                x_early[:, : 2 * split] = jnp.concatenate([noise, jnp.zeros_like(noise)], axis=1).astype(BF16)
            with jax.named_scope("gram"):
                for part in range(2):
                    at = slice(part * (width // 2), (part + 1) * (width // 2))
                    probe = jnp.concatenate([both[split : 2 * split, at], both[depth:, at]], axis=0)
                    gram[part] = nt(probe, both[:depth, at])
                square = gram[0] + gram[1]
                sums = square[split:]
                wmean = sums[0:1] * (1.0 / width)
                cross = (sums[1:2] + sums[2:3] + sums[3:4]) * 2.0
                high, low = halves(square[:split])
                own_gram[:split, :] = high[:, : 2 * split]
                own_gram[split:, :] = low[:, : 2 * split]
                late_mean[...] = wmean[:, : 2 * split]
                pair_high = jnp.concatenate([high, high], axis=0)
                pair_low = jnp.concatenate([low, low], axis=0)
                for k in range(0, tokens, block):
                    at = slice(k, k + block)
                    x = x_early[at, :]
                    y = nt(x, pair_high) + nt(x, pair_low)
                    mean = jnp.sum(x.astype(F32) * wmean, axis=-1, keepdims=True)
                    base[0, at, :] = jnp.broadcast_to(mean, (block, 128))
                    base[2, at, :] = 2.0 * y + cross[:, : 2 * split]

    with jax.named_scope("early"):
        step = 256
        for k in range(0, width, step):
            at = slice(k, k + step)
            part = jnp.dot(x_early[...], both[:depth, at], preferred_element_type=F32) + center[0, :, at]
            early_ref[:, at] = part * center[1, :, at]
            square = part * part
            square = square[:, :128] + square[:, 128:]
            if k == 0:
                base[1] = square
            else:
                base[1] = base[1] + square

    def drain(slot, own_piece):
        total = (frames if slot == 0 else reach - frames) * chunks
        for ci in range(n_c):
            less = own_piece & (c == ci)

            @pl.when(less)
            def _():
                part = msg.at[: total - 1]
                pltpu.make_async_copy(part, part, s_sem.at[slot, ci]).wait()

            @pl.when(jnp.logical_not(less))
            def _():
                part = msg.at[:total]
                pltpu.make_async_copy(part, part, s_sem.at[slot, ci]).wait()

    with jax.named_scope("drain"):
        drain(0, own_main)

        @pl.when(more)
        def _():
            drain(1, own_carry)

    with jax.named_scope("recv"):

        @pl.when(carried)
        def _():
            pltpu.make_async_copy(got.at[1], got.at[1], r_sem.at[1]).wait()

        pltpu.make_async_copy(got.at[0], got.at[0], r_sem.at[0]).wait()

    with jax.named_scope("assemble"):
        odd = lane // (2 * z) % 2 == 1

        def strip(slot, si):
            v = got[slot, si, :per, :].astype(F32)
            parts = [v[k : k + 8] for k in range(0, per, 8)]
            if si > 0:
                parts[0] = parts[0] + jnp.where(odd, 0.0, got[slot, si - 1, per:, :].astype(F32))
            if si < n_s - 1:
                parts[-1] = parts[-1] + jnp.where(odd, got[slot, si + 1, per:, :].astype(F32), 0.0)
            return jnp.concatenate(parts, axis=0)

        for si in range(n_s):
            stack[si * per : (si + 1) * per, :] = strip(0, si) + bias_row[...]

        @pl.when(carried)
        def _():
            for si in range(n_s):
                at = slice(si * per, (si + 1) * per)
                stack[at, :] = stack[at, :] + strip(1, si)

        placed = jnp.dot(order[...], stack[...].astype(BF16), preferred_element_type=F32)
        turned = pltpu.roll(placed, 64, 1)
        low = lax.broadcasted_iota(jnp.int32, (n, 128), 1) < 64
        twice = [jnp.where(low, placed, turned), jnp.where(low, turned, placed)]
        for h in range(2):
            lhs_ref[h * n : (h + 1) * n, : 2 * split] = twice[h].astype(BF16)

    with jax.named_scope("stats"):
        for k in range(0, tokens, block):
            at = slice(k, k + block)
            x = lhs_ref[at, : 2 * split]
            y = jnp.dot(x, own_gram[...], preferred_element_type=F32) + base[2, at, :]
            wide_lane = lax.broadcasted_iota(jnp.int32, (block, 128), 1)
            x = jnp.where(wide_lane < split, 0.0, x.astype(F32))
            mean = jnp.sum(x * late_mean[...], axis=-1, keepdims=True) + base[0, at, :]
            power = jnp.sum(x * y + base[1, at, :], axis=-1, keepdims=True)
            variance = jnp.maximum(power * (1.0 / width) - mean * mean, 0.0)
            inv_ref[at, :] = lax.rsqrt(variance + 1e-06)
            high = mean.astype(BF16).astype(F32)
            pair = jnp.where(wide_lane < 2, high, mean - high)
            lhs_ref[at, 2 * split :] = jnp.where(wide_lane < 4, -pair, 0.0).astype(BF16)


def write_kernel(lhs, late, early, inv, shift, out, buf, sem):
    width = buf.shape[1]
    wide = 512 if width % 512 == 0 else width
    step = min(wide, 256)
    copies = []
    for k in range(0, width, wide):
        for q in range(k, k + wide, step):
            at = slice(q, q + step)
            part = jnp.dot(lhs[:, : late.shape[0]], late[:, at], preferred_element_type=F32)
            factor = jnp.concatenate([inv[...]] * (step // 128), axis=1)
            buf[:, at] = ((part + early[:, at]) * factor + shift[:, at]).astype(BF16)
        copy = pltpu.make_async_copy(buf.at[:, k : k + wide], out.at[:, k : k + wide], sem.at[k // wide])
        copy.start()
        copies.append(copy)
    for copy in copies:
        copy.wait()


def fast(
    section_input, norm_gain, conv_weight, conv_bias, mean_weight, mean_bias, noisy_tokens,
    mask_tokens, patch_weight, patch_bias, context_weight, context_bias, norm_shift, norm_scale,
):
    frames, height, columns, channels = section_input.shape
    n_c, n_s, n_t = lax.axis_size("cfg"), lax.axis_size("seq"), lax.axis_size("tile")
    z = mean_weight.shape[1]
    tokens, width = noisy_tokens.shape[0], patch_weight.shape[1]
    shard_rows = tokens // (n_s * columns // 2)
    half = height // n_c
    count = half * columns
    chunks = half // 2 // shard_rows
    reach = frames + K - 1
    per = (columns // 2 + 1) * 8
    depth = patch_weight.shape[0] + context_weight.shape[0]
    split = 4 * z
    n = n_s * columns // 2 * 8
    vmem = pl.BlockSpec(memory_space=pltpu.VMEM)
    hbm = pl.BlockSpec(memory_space=pltpu.HBM)
    args = (
        section_input, conv_weight.T, norm_gain, mean_weight.T, conv_bias[None], mean_bias[None],
        noisy_tokens.T, mask_tokens, patch_weight, context_weight, patch_bias[None], context_bias[None],
        norm_scale[None],
    )
    prepared = pl.pallas_call(
        functools.partial(send_kernel, (n_c, n_s, n_t, shard_rows)),
        out_shape=(
            pltpu.VMEM((tokens, 2 * split + 128), BF16),
            pltpu.VMEM((2 * split + 16, width), BF16),
            pltpu.VMEM((tokens, width), F32),
            pltpu.VMEM((tokens, 128), F32),
        ),
        in_specs=[hbm] * len(args),
        out_specs=(vmem,) * 4,
        scratch_shapes=[
            pltpu.VMEM(conv_weight.shape[::-1], BF16),
            pltpu.VMEM((channels,), F32),
            pltpu.VMEM(mean_weight.shape[::-1], F32),
            pltpu.VMEM((1, conv_bias.shape[0]), F32),
            pltpu.VMEM((1, z), F32),
            pltpu.VMEM((1, width), F32),
            pltpu.VMEM((1, width), F32),
            pltpu.VMEM((1, width), F32),
            pltpu.VMEM((16 * z, frames * K * channels), BF16),
            pltpu.VMEM((frames, half + 2, columns, channels), BF16),
            pltpu.VMEM((frames, (half + 2) * columns, channels), F32),
            pltpu.VMEM((frames, count, 128), F32),
            pltpu.VMEM((frames, count, 128), F32),
            pltpu.VMEM((n, 128), F32),
            pltpu.VMEM((reach * chunks, per, 128), BF16),
            pltpu.VMEM((2, n_s, per, 128), BF16),
            pltpu.VMEM((split, width), BF16),
            pltpu.VMEM((depth + 16, width), BF16),
            pltpu.VMEM(noisy_tokens.shape[::-1], BF16),
            pltpu.VMEM((2, split + 16, depth), F32),
            pltpu.VMEM((2 * split, 2 * split), BF16),
            pltpu.VMEM((n, n), BF16),
            pltpu.VMEM((split, split), BF16),
            pltpu.VMEM((1, 128), F32),
            pltpu.VMEM((2, 1, width), F32),
            pltpu.VMEM((1, 128), F32),
            pltpu.VMEM((tokens, depth), BF16),
            pltpu.VMEM((3, tokens, 128), F32),
            pltpu.SemaphoreType.DMA((15,)),
            pltpu.SemaphoreType.DMA((2, n_c)),
            pltpu.SemaphoreType.DMA((2,)),
        ],
        compiler_params=pltpu.CompilerParams(
            collective_id=0, has_side_effects=True, vmem_limit_bytes=32 * 2**20
        ),
        name="send",
    )(*(pltpu.with_memory_space_constraint(v, pltpu.HBM) for v in args))
    return pl.pallas_call(
        write_kernel,
        out_shape=jax.ShapeDtypeStruct((tokens, width), BF16),
        in_specs=[vmem] * 5,
        out_specs=hbm,
        scratch_shapes=[pltpu.VMEM((tokens, width), BF16), pltpu.SemaphoreType.DMA((max(1, width // 512),))],
        compiler_params=pltpu.CompilerParams(vmem_limit_bytes=24 * 2**20),
        name="write",
    )(*prepared, norm_shift[None])


def choose(*args):
    n_c, n_s, n_t = lax.axis_size("cfg"), lax.axis_size("seq"), lax.axis_size("tile")
    frames, height, columns, _ = args[0].shape
    rows = args[6].shape[0] // (n_s * columns // 2)
    fits = columns == 8 and args[4].shape[1] == 16 and frames == 2 and rows == 16
    fits = fits and height // n_c == 4 * rows
    return fast(*args) if fits else body(*args)


def solution(mesh):
    placed = (P("tile", None, "seq", None),) + (P(),) * 5
    placed = placed + (P(("seq", "tile"), None),) * 2 + (P(),) * 6
    return jax.shard_map(
        choose, mesh=mesh, in_specs=placed, out_specs=P(("seq", "tile"), None), check_vma=False
    )
```

```python
import functools

import jax
import jax.numpy as jnp
from jax import lax
from jax.experimental import pallas as pl
from jax.experimental.pallas import tpu as pltpu
from jax.sharding import PartitionSpec as P

K = 3
MESH = pl.DeviceIdType.MESH
F32 = jnp.float32
BF16 = jnp.bfloat16


def ones_where(shape, test):
    i = lax.broadcasted_iota(jnp.int32, shape, 0)
    j = lax.broadcasted_iota(jnp.int32, shape, 1)
    return jnp.where(test(i, j), 1.0, 0.0)


def nt(x, y):
    return lax.dot_general(x, y, (((1,), (1,)), ((), ())), preferred_element_type=F32)


def fold_weights(cw_ref, mw_ref, wt):
    z, zo = mw_ref.shape
    mw = mw_ref[...]
    high = mw.astype(BF16)
    low = (mw - high.astype(F32)).astype(BF16)
    spread = ones_where((4 * z, z), lambda i, j: i % z == j).astype(BF16)
    copier = ones_where((zo, K * zo), lambda i, j: j % zo == i).astype(BF16)

    def right_slot(i, j):
        slot, e = i // z, j // zo
        return ((slot == 0) & (e == 1)) | ((slot == 2) & (e == 0)) | ((slot == 3) & (e == 2))

    keep = ones_where((4 * z, K * zo), right_slot)
    parts = []
    for part in (high, low):
        tall = jnp.dot(spread, part, preferred_element_type=F32).astype(BF16)
        parts.append((jnp.dot(tall, copier, preferred_element_type=F32) * keep).astype(BF16))
    parts = jnp.concatenate(parts, axis=0)
    nothing = jnp.zeros((z, wt.shape[2]), BF16)
    for a in range(K):
        for b in range(K):
            at = (a * K + b) * K * zo
            rhs = cw_ref[at : at + K * zo, :]
            res = jnp.dot(parts, rhs, preferred_element_type=F32)
            res = (res[: 4 * z] + res[4 * z :]).astype(BF16)
            for f in range(2):
                for slot in range(4):
                    row = slot * 4 * z + (f + 2 - a) * z
                    wt[f * K + b, row : row + z, :] = res[slot * z : (slot + 1) * z]
    for b in range(K):
        for slot in range(4):
            row = slot * 4 * z
            wt[b, row + 3 * z : row + 4 * z, :] = nothing
            wt[K + b, row : row + z, :] = nothing


def fold_bias(mw_ref, cb_ref, mb_ref):
    z = mw_ref.shape[0]
    copier = ones_where((128, z), lambda i, j: i % z == j)
    exact = functools.partial(
        lax.dot_general, dimension_numbers=(((1,), (1,)), ((), ())),
        precision=lax.Precision.HIGHEST, preferred_element_type=F32,
    )
    return exact(exact(cb_ref[...], mw_ref[...]) + mb_ref[...], copier)


def head_kernel(
    sizes, x_hbm, cw_ref, gain_ref, mw_ref, cb_ref, mb_ref, out_ref,
    wt, xin, actf, acc, edge, pk, rs_send, ls_send, ca_send, rs_got, ls_got, ca_got, patch,
    in_sem, s1_sem, r1_sem, s2_sem, r2_sem,
):
    n_c, n_s, n_t, shard_rows = sizes
    c, s, t = lax.axis_index("cfg"), lax.axis_index("seq"), lax.axis_index("tile")
    frames, height, columns, channels = x_hbm.shape
    half = height // n_c
    pairs = half // 2
    z = 16
    chunks = pairs // shard_rows
    chunk_tokens = shard_rows * (columns // 2)

    def dev(ci, si, ti):
        return {"cfg": ci, "seq": si, "tile": ti}

    load = pltpu.make_async_copy(
        x_hbm.at[:, pl.ds(c * (half - 1), half + 1)],
        xin.at[:, pl.ds(1 - c, half + 1)],
        in_sem,
    )
    load.start()

    barrier = pltpu.get_barrier_semaphore()
    links = [(1, 0), (-1, 0), (0, 1), (1, 1), (-1, 1)]

    def there(ds, dt, sign):
        si, ti = s + sign * ds, t + sign * dt
        return (si >= 0) & (si < n_s) & (ti >= 0) & (ti < n_t), si, ti

    expect = jnp.int32(0)
    for ds, dt in links:
        ok, si, ti = there(ds, dt, -1)

        @pl.when(ok)
        def _():
            pl.semaphore_signal(barrier, inc=1, device_id=dev(c, si, ti), device_id_type=MESH)

        ok, _, _ = there(ds, dt, 1)
        expect = expect + ok.astype(jnp.int32)

    first = (s * n_t + t) * shard_rows
    src_t = first // (height // 2) // frames
    src_c = first % (height // 2) // pairs
    for si in range(n_s):
        mine = (src_c == c) & (src_t == t) & (s == si)

        @pl.when(jnp.logical_not(mine))
        def _():
            pl.semaphore_signal(barrier, inc=1, device_id=dev(src_c, si, src_t), device_id_type=MESH)

    own = (src_c == c) & (src_t == t)
    expect = expect + frames * chunks * n_c - own.astype(jnp.int32)

    fold_weights(cw_ref, mw_ref, wt)
    bias = fold_bias(mw_ref, cb_ref, mb_ref)

    zero_row = jnp.zeros((frames, 1, columns, channels), BF16)

    @pl.when(c == 0)
    def _():
        xin[:, 0:1] = zero_row

    @pl.when(c == n_c - 1)
    def _():
        xin[:, half + 1 : half + 2] = zero_row

    load.wait()
    gain = gain_ref[...].reshape(1, channels)
    step_rows = 6 if (half + 2) % 6 == 0 else 2
    for f in range(frames):

        @pl.loop(0, (half + 2) // step_rows)
        def _(r):
            v = xin[f, pl.ds(r * step_rows, step_rows)].astype(F32)
            v = v.reshape(step_rows * columns, channels)
            energy = jnp.sum(v * v, axis=-1, keepdims=True) * (1.0 / channels)
            v = v * lax.rsqrt(energy + 1e-06) * gain
            v = v / (1.0 + jnp.exp(-v))
            at = pl.multiple_of(r * (step_rows * columns), step_rows * columns)
            actf[f, pl.ds(at, step_rows * columns), :] = v

    rows = half * columns
    for m in range(2):
        lo = m * (rows // 2)
        total = None
        for f in range(frames):
            for b in range(K):
                lhs = actf[f, lo + b * columns : lo + b * columns + rows // 2, :].astype(BF16)
                term = nt(lhs, wt[f * K + b])
                total = term if total is None else total + term
        acc[lo : lo + rows // 2, :] = total[:, :128]
        edge[lo : lo + rows // 2, :] = total[:, 128:]

    q = edge[...]
    w_at = lax.broadcasted_iota(jnp.int32, (rows, 128), 0) % columns
    right = jnp.where(w_at == 0, 0.0, pltpu.roll(q, 1, 0))
    left = jnp.where(w_at == columns - 1, 0.0, pltpu.roll(q, rows - 1, 0))
    acc[...] = acc[...] + right + pltpu.roll(left, 64, 1)
    rs_send[...] = edge[pl.ds(columns - 1, half, stride=columns), :].astype(BF16)
    ls_send[...] = edge[pl.ds(0, half, stride=columns), :].astype(BF16)
    quarter = rows // 4
    lane = lax.broadcasted_iota(jnp.int32, (quarter, 128), 1)
    packed = jnp.zeros((quarter, 128), F32)
    for k in range(4):
        part = pltpu.roll(acc[k * quarter : (k + 1) * quarter, :], (k * 32 + 128 - 32) % 128, 1)
        packed = jnp.where(lane // 32 == k, part, packed)
    ca_send[...] = packed.astype(BF16)

    pl.semaphore_wait(barrier, expect)

    bufs = {1: (rs_send, rs_got), -1: (ls_send, ls_got), 0: (ca_send, ca_got)}

    def link_copy(i, sign):
        ds, dt = links[i]
        ok, si, ti = there(ds, dt, sign)
        src, dst = bufs[ds]
        if ds != 0:
            dst = dst.at[dt]
        return ok, pltpu.make_async_remote_copy(
            src_ref=src, dst_ref=dst, send_sem=s1_sem.at[i], recv_sem=r1_sem.at[i],
            device_id=dev(c, si, ti), device_id_type=MESH,
        )

    for i in (2, 3, 4, 0, 1):
        ok, copy = link_copy(i, 1)

        @pl.when(ok)
        def _():
            copy.start()

    for i in (0, 1, 3, 4, 2):
        ds, dt = links[i]
        ok, copy = link_copy(i, -1)

        @pl.when(ok)
        def _():
            copy.wait_recv()
            if ds == 0:
                got = ca_got[...].astype(F32)
                for k in range(4):
                    acc[k * quarter : (k + 1) * quarter, :] += pltpu.roll(got, (128 - 32 * k) % 128, 1)
            else:
                got = bufs[ds][1][dt].astype(F32)
                turn = (128 - 32 * dt - (64 if ds < 0 else 0)) % 128
                if turn:
                    got = pltpu.roll(got, turn, 1)
                at = pl.ds(0 if ds > 0 else columns - 1, half, stride=columns)
                acc[at, :] = acc[at, :] + got

    total = acc[...] + bias
    by_row = total.reshape(pairs, 2, columns, 128)
    even = by_row[:, 0].reshape(pairs * columns, 128)
    odd = by_row[:, 1].reshape(pairs * columns, 128)
    lane = lax.broadcasted_iota(jnp.int32, (pairs * columns, 128), 1)
    mixed = jnp.where(
        lane < 16, even,
        jnp.where(
            lane < 32, pltpu.roll(odd, 16, 1),
            jnp.where(lane < 48, pltpu.roll(even, 16, 1), pltpu.roll(odd, 32, 1)),
        ),
    )
    pk[...] = mixed
    tokens = pairs * columns // 2
    left_half = pk[pl.ds(0, tokens, stride=2), :]
    right_half = pk[pl.ds(1, tokens, stride=2), :]
    lane = lax.broadcasted_iota(jnp.int32, (tokens, 128), 1)
    for f in range(frames):
        one = left_half if f == 0 else pltpu.roll(left_half, 128 - 32 * f, 1)
        two = pltpu.roll(right_half, (32 - 32 * f) % 128, 1) if f != 1 else right_half
        both = jnp.where(lane < 32, one, two)
        for m in range(chunks):
            patch[f * chunks + m] = both[m * chunk_tokens : (m + 1) * chunk_tokens, :64].astype(BF16)

    def patch_copy(f, m, ci):
        shard = ((t * frames + f) * (height // 2) + c * pairs) // shard_rows + m
        si, ti = shard // n_t, shard % n_t
        mine = (si == s) & (ti == t) & (c == ci)
        piece = f * chunks + m
        local = pltpu.make_async_copy(patch.at[piece], out_ref.at[s], r2_sem.at[s])
        away = pltpu.make_async_remote_copy(
            src_ref=patch.at[piece], dst_ref=out_ref.at[s],
            send_sem=s2_sem.at[piece * n_c + ci], recv_sem=r2_sem.at[s],
            device_id=dev(ci, si, ti), device_id_type=MESH,
        )
        return mine, local, away

    every = [(f, m, ci) for f in range(frames) for m in range(chunks) for ci in range(n_c)]
    for item in every:
        mine, local, away = patch_copy(*item)

        @pl.when(mine)
        def _():
            local.start()

        @pl.when(jnp.logical_not(mine))
        def _():
            away.start()

    for si in range(n_s):
        pltpu.make_async_copy(patch.at[0], out_ref.at[si], r2_sem.at[si]).wait()
    for i in range(5):
        ok, copy = link_copy(i, 1)

        @pl.when(ok)
        def _():
            copy.wait_send()

    for item in every:
        mine, _, away = patch_copy(*item)

        @pl.when(jnp.logical_not(mine))
        def _():
            away.wait_send()


def tail_kernel(noisy, mask, lat, pw, cw, pb, cb, shift, scale, out, comb, both, inv_ref, mean_ref, sems):
    split = lat.shape[-1]
    width = comb.shape[1]
    step = 512
    z = split // 4

    @pl.when(pl.program_id(0) == 0)
    def _():
        upper = pltpu.make_async_copy(pw, both.at[:split], sems.at[0])
        lower = pltpu.make_async_copy(cw, both.at[split:], sems.at[1])
        upper.start()
        lower.start()
        upper.wait()
        lower.wait()

    parts = comb.shape[0] // out.shape[0]

    @pl.when(pl.program_id(0) % parts == 0)
    def _():
        perm = ones_where(
            (split, split), lambda i, j: j == (i % z) * 4 + (i // z % 2) * 2 + i // (2 * z)
        ).astype(BF16)
        if len(lat.shape) == 3:
            strips, per, _ = lat.shape
            tokens = lat[...].reshape(strips * per, split)
            n, cols = strips * per, 4
            order = ones_where(
                (n, n),
                lambda i, j: j == (i // cols % strips) * per + i // (cols * strips) * cols + i % cols,
            ).astype(BF16)
            tokens = jnp.dot(order, tokens, preferred_element_type=F32).astype(BF16)
        else:
            tokens = lat[...]
        tokens = jnp.dot(tokens, perm, preferred_element_type=F32)
        own = noisy[...].astype(F32).T
        lhs = jnp.concatenate([own, tokens, mask[...].astype(F32)], axis=1).astype(BF16)
        total = None
        for k in range(0, width, step):
            at = slice(k, k + step)
            part = jnp.dot(lhs, both[:, at], preferred_element_type=F32)
            part = part + (pb[:, at] + cb[:, at])
            comb[:, at] = part
            term = jnp.sum(part, axis=-1, keepdims=True)
            total = term if total is None else total + term
        mean = total * (1.0 / width)
        square = None
        for k in range(0, width, step):
            d = comb[:, k : k + step] - mean
            term = jnp.sum(d * d, axis=-1, keepdims=True)
            square = term if square is None else square + term
        mean_ref[...] = jnp.broadcast_to(mean, mean_ref.shape)
        inv_ref[...] = jnp.broadcast_to(lax.rsqrt(square * (1.0 / width) + 1e-06), inv_ref.shape)

    rows = out.shape[0]
    mine = pl.ds(pl.multiple_of(pl.program_id(0) % parts * rows, rows), rows)
    mean, inv = mean_ref[mine, :1], inv_ref[mine, :1]
    for k in range(0, width, step):
        at = slice(k, k + step)
        out[:, at] = ((comb[mine, at] - mean) * inv * (1.0 + scale[:, at]) + shift[:, at]).astype(BF16)


def body(
    section_input, norm_gain, conv_weight, conv_bias, mean_weight, mean_bias, noisy_tokens,
    mask_tokens, patch_weight, patch_bias, context_weight, context_bias, norm_shift, norm_scale,
):
    frames, height, columns, channels = section_input.shape
    n_c, n_s, n_t = lax.axis_size("cfg"), lax.axis_size("seq"), lax.axis_size("tile")
    z = mean_weight.shape[1]
    tokens = noisy_tokens.shape[0]
    shard_rows = tokens // (n_s * columns // 2)
    half = height // n_c
    rows = half * columns
    chunks = half // 2 // shard_rows
    chunk_tokens = shard_rows * (columns // 2)
    vmem = pl.BlockSpec(memory_space=pltpu.VMEM)
    arrived = pl.pallas_call(
        functools.partial(head_kernel, (n_c, n_s, n_t, shard_rows)),
        out_shape=jax.ShapeDtypeStruct((n_s, chunk_tokens, 4 * z), BF16),
        in_specs=[pl.BlockSpec(memory_space=pltpu.HBM)] + [vmem] * 5,
        out_specs=vmem,
        scratch_shapes=[
            pltpu.VMEM((frames * K, 16 * z, channels), BF16),
            pltpu.VMEM((frames, half + 2, columns, channels), BF16),
            pltpu.VMEM((frames, (half + 2) * columns, channels), F32),
            pltpu.VMEM((rows, 128), F32),
            pltpu.VMEM((rows, 128), F32),
            pltpu.VMEM((rows // 2, 128), F32),
            pltpu.VMEM((half, 128), BF16),
            pltpu.VMEM((half, 128), BF16),
            pltpu.VMEM((rows // 4, 128), BF16),
            pltpu.VMEM((2, half, 128), BF16),
            pltpu.VMEM((2, half, 128), BF16),
            pltpu.VMEM((rows // 4, 128), BF16),
            pltpu.VMEM((frames * chunks, chunk_tokens, 4 * z), BF16),
            pltpu.SemaphoreType.DMA,
            pltpu.SemaphoreType.DMA((5,)),
            pltpu.SemaphoreType.DMA((5,)),
            pltpu.SemaphoreType.DMA((frames * chunks * n_c,)),
            pltpu.SemaphoreType.DMA((n_s,)),
        ],
        compiler_params=pltpu.CompilerParams(collective_id=0, has_side_effects=True),
        name="head",
    )(
        section_input, conv_weight.T, norm_gain, mean_weight.T, conv_bias[None], mean_bias[None]
    )
    width = patch_weight.shape[1]
    block = min(tokens, 256)
    per = block // n_s
    if per % 16 == 0 and columns == 8:
        lat = arrived
        lat_spec = pl.BlockSpec((n_s, per, 4 * z), lambda i: (0, i // parts, 0))
    else:
        lat = arrived.reshape(n_s, shard_rows, columns // 2, 4 * z).transpose(1, 0, 2, 3)
        lat = lat.reshape(tokens, 4 * z)
        lat_spec = pl.BlockSpec((block, 4 * z), lambda i: (i // parts, 0))
    parts = 2 if block % 32 == 0 else 1
    tok = lambda n: pl.BlockSpec((block, n), lambda i: (i // parts, 0))
    full = lambda a: pl.BlockSpec(a.shape, lambda i: (0, 0))
    hbm = pl.BlockSpec(memory_space=pl.ANY)
    depth = patch_weight.shape[0] + context_weight.shape[0]
    vecs = [v[None] for v in (patch_bias, context_bias, norm_shift, norm_scale)]
    return pl.pallas_call(
        tail_kernel,
        out_shape=jax.ShapeDtypeStruct((tokens, width), BF16),
        grid=(tokens // block * parts,),
        in_specs=[
            pl.BlockSpec((noisy_tokens.shape[1], block), lambda i: (0, i // parts)),
            tok(mask_tokens.shape[1]), lat_spec, hbm, hbm,
        ]
        + [full(v) for v in vecs],
        out_specs=pl.BlockSpec((block // parts, width), lambda i: (i, 0)),
        scratch_shapes=[
            pltpu.VMEM((block, width), F32),
            pltpu.VMEM((depth, width), BF16),
            pltpu.VMEM((block, 128), F32),
            pltpu.VMEM((block, 128), F32),
            pltpu.SemaphoreType.DMA((2,)),
        ],
        name="tail",
    )(noisy_tokens.T, mask_tokens, lat, patch_weight, context_weight, *vecs)


def fold_parts(mw_ref):
    z, zo = mw_ref.shape
    wide = jnp.concatenate([mw_ref[...]] * K, axis=1)
    tap = lax.broadcasted_iota(jnp.int32, wide.shape, 1) // zo
    tall = jnp.concatenate([jnp.where(tap == e, wide, 0.0) for e in (1, 0, 2)], axis=0)
    high = tall.astype(BF16).astype(F32)
    return jnp.concatenate([high, tall - high], axis=1).astype(BF16)


def fold_taps(cw_ref, parts, wt, z, outer):
    channels = cw_ref.shape[1]
    size = parts.shape[1] // 2
    for a in outer:
        for b in range(K):
            at = (a * K + b) * size
            tap = cw_ref[at : at + size, :]
            res = jnp.dot(parts, jnp.concatenate([tap, tap], axis=0), preferred_element_type=F32)
            res = res.astype(BF16)
            for f in range(2):
                for k, slot in enumerate((0, 2, 3)):
                    row = slot * 4 * z + (f + 2 - a) * z
                    wt[row : row + z, (f * K + b) * channels : (f * K + b + 1) * channels] = res[
                        k * z : (k + 1) * z
                    ]


def fold_zeros(wt, z, channels):
    deep = K * channels
    for slot in range(4):
        row = slot * 4 * z
        if slot == 1:
            wt[row : row + 4 * z, :] = jnp.zeros((4 * z, 2 * deep), BF16)
        else:
            wt[row + 3 * z : row + 4 * z, :deep] = jnp.zeros((z, deep), BF16)
            wt[row : row + z, deep:] = jnp.zeros((z, deep), BF16)


def halves(v):
    high = v.astype(BF16)
    return high, (v - high.astype(F32)).astype(BF16)


def send_kernel(
    sizes, x_hbm, cw_hbm, gain_hbm, mw_hbm, cb_hbm, mb_hbm, noisy_hbm, mask_hbm, pw_hbm, xw_hbm, pb_hbm,
    xb_hbm, scale_hbm, lhs_ref, late_ref, early_ref, inv_ref,
    cwt, gain_ref, mw_ref, cb_ref, mb_ref, pb_ref, xb_ref, scale_ref, wt, xin, actf, cen, edge, msg, got,
    lat_w, both, own, gram, own_gram, order, swap, bias_row, center, late_mean, x_early, base, in_sem, s_sem, r_sem,
):
    n_c, n_s, n_t, shard_rows = sizes
    c, s, t = lax.axis_index("cfg"), lax.axis_index("seq"), lax.axis_index("tile")
    frames, height, columns, channels = x_hbm.shape
    half = height // n_c
    pairs = half // 2
    z = mw_ref.shape[0]
    chunks = pairs // shard_rows
    reach = frames + K - 1
    split = 4 * z
    width = late_ref.shape[1]
    tokens = lhs_ref.shape[0]
    depth = pw_hbm.shape[0] + xw_hbm.shape[0]

    def dev(ci, si, ti):
        return {"cfg": ci, "seq": si, "tile": ti}

    cut = half // 2 + 2
    start = c * (half - 1)
    xs = [
        [
            pltpu.make_async_copy(
                x_hbm.at[f, pl.ds(start + lo, size)],
                xin.at[f, pl.ds(1 - c + lo, size)],
                in_sem.at[i * frames + f],
            )
            for f in range(frames)
        ]
        for i, (lo, size) in enumerate(((0, cut), (cut, half + 1 - cut)))
    ]
    third = cw_hbm.shape[0] // K
    taps = [
        pltpu.make_async_copy(
            cw_hbm.at[a * third : (a + 1) * third], cwt.at[a * third : (a + 1) * third], in_sem.at[4 + a]
        )
        for a in range(K)
    ]
    small = [
        pltpu.make_async_copy(src, dst, in_sem.at[7 + i])
        for i, (src, dst) in enumerate(
            ((gain_hbm, gain_ref), (mw_hbm, mw_ref), (cb_hbm, cb_ref), (mb_hbm, mb_ref))
        )
    ]
    later = [
        pltpu.make_async_copy(src, dst, in_sem.at[11 + i])
        for i, (src, dst) in enumerate(
            (
                (pb_hbm, pb_ref), (xb_hbm, xb_ref), (scale_hbm, scale_ref), (noisy_hbm, own),
                (mask_hbm, x_early.at[:, 2 * split :]), (xw_hbm.at[:split], lat_w),
                (pw_hbm, both.at[:split]), (xw_hbm.at[split:], both.at[2 * split : depth]),
            )
        )
    ]
    small[1].start()
    for load in taps:
        load.start()
    for load in xs[0]:
        load.start()
    small[0].start()
    for load in xs[1]:
        load.start()
    small[2].start()
    small[3].start()

    barrier = pltpu.get_barrier_semaphore()
    first = (s * n_t + t) * shard_rows
    frame = first // (height // 2)
    src_t = frame // frames
    src_c = first % (height // 2) // pairs
    carried = (src_t > 0) & (frame % frames < K - 1)
    for si in range(n_s):
        for back in range(2):
            mine = (src_c == c) & (src_t - back == t) & (s == si)
            wanted = jnp.logical_not(mine)
            if back:
                wanted = wanted & carried

            @pl.when(wanted)
            def _():
                pl.semaphore_signal(
                    barrier, inc=1, device_id=dev(src_c, si, src_t - back), device_id_type=MESH
                )

    def place(g, m):
        shard = ((t * frames + g) * (height // 2) + c * pairs) // shard_rows + m
        return shard // n_t, shard % n_t

    own_main = (src_c == c) & (src_t == t)
    own_carry = (src_c == c) & (src_t - 1 == t) & carried
    more = t + 1 < n_t
    expect = frames * chunks * n_c - own_main.astype(jnp.int32)
    rest = (reach - frames) * chunks * n_c - own_carry.astype(jnp.int32)
    expect = expect + jnp.where(more, rest, 0)

    zero_row = jnp.zeros((frames, 1, columns, channels), BF16)

    @pl.when(c == 0)
    def _():
        xin[:, 0:1] = zero_row

    @pl.when(c == n_c - 1)
    def _():
        xin[:, half + 1 : half + 2] = zero_row

    def activate(lo, hi):
        step = 2
        for f in range(frames):
            for r in range(lo, hi, step):
                v = xin[f, r : r + step].astype(F32).reshape(step * columns, channels)
                energy = jnp.sum(v * v, axis=-1, keepdims=True)
                v = v * lax.rsqrt(energy + 1e-06 * channels) * gain
                actf[f, r * columns : (r + step) * columns, :] = v + v * jnp.tanh(v)

    count = half * columns // 2

    def convolve(m):
        lo = m * count
        for f in range(frames):
            taps = [actf[f, lo + b * columns : lo + b * columns + count, :].astype(BF16) for b in range(K)]
            total = nt(jnp.concatenate(taps, axis=1), wt[:, f * K * channels : (f + 1) * K * channels])
            cen[f, lo : lo + count, :] = total[:, :128]
            edge[f, lo : lo + count, :] = total[:, 128:]

    def both_frames(ref, at):
        v = ref[0, pl.ds(at, 8, stride=2 * columns), :]
        for f in range(1, frames):
            v = v + ref[f, pl.ds(at, 8, stride=2 * columns), :]
        return v

    lane = lax.broadcasted_iota(jnp.int32, (8, 128), 1)
    upper = lane >= 64
    one = lane // z % 2 == 1
    two = lane // z % 4 >= 2

    def pack(m):
        cols = {}
        for a in range(2):
            mids, rights, lefts = [], [], []
            for w in range(columns):
                starts = [((m * shard_rows + h * 8) * 2 + a) * columns + w for h in range(2)]
                c0, c1 = (both_frames(cen, at) for at in starts)
                e0, e1 = (both_frames(edge, at) for at in starts)
                mids.append(jnp.where(upper, pltpu.roll(c1, 64, 1), c0))
                turned = pltpu.roll(jnp.where(upper, e0, e1), 64, 1)
                rights.append(jnp.where(upper, turned, e0))
                lefts.append(jnp.where(upper, e1, turned))
            for w in range(columns):
                v = mids[w]
                if w > 0:
                    v = v + rights[w - 1]
                if w < columns - 1:
                    v = v + lefts[w + 1]
                cols[a, w] = v
            cols[a, columns] = rights[columns - 1]
            cols[a, columns + 1] = lefts[0]
        for j in range(columns // 2 + 1):
            p = [cols[a, 2 * j + b] for b in range(2) for a in range(2)]
            q = [None] * 4
            for k in (0, 2):
                q[k] = jnp.where(one, pltpu.roll(p[k + 1], z, 1), p[k])
                q[k + 1] = jnp.where(one, p[k + 1], pltpu.roll(p[k], 128 - z, 1))
            for k in range(2):
                low = jnp.where(two, pltpu.roll(q[k + 2], 2 * z, 1), q[k])
                high = jnp.where(two, q[k + 2], pltpu.roll(q[k], 128 - 2 * z, 1))
                msg[k * chunks + m, j * 8 : j * 8 + 8, :] = low.astype(BF16)
                msg[(k + 2) * chunks + m, j * 8 : j * 8 + 8, :] = high.astype(BF16)

    def send(m):
        def post(g):
            si, ti = place(g, m)
            here = (si == s) & (ti == t)
            slot = g // frames
            src, dst = msg.at[g * chunks + m], got.at[slot, s]
            for ci in range(n_c):

                @pl.when(here & (c == ci))
                def _():
                    pltpu.make_async_copy(src, dst, r_sem.at[slot]).start()

                @pl.when(jnp.logical_not(here & (c == ci)))
                def _():
                    pltpu.make_async_remote_copy(
                        src_ref=src, dst_ref=dst, send_sem=s_sem.at[slot, ci], recv_sem=r_sem.at[slot],
                        device_id=dev(ci, si, ti), device_id_type=MESH,
                    ).start()

        for g in range(frames):
            post(g)

        @pl.when(more)
        def _():
            for g in range(frames, reach):
                post(g)

    per = columns // 2 * 8
    n = n_s * per
    cols = columns // 2
    with jax.named_scope("tables"):
        i = lax.broadcasted_iota(jnp.int32, (n, n), 0)
        j = lax.broadcasted_iota(jnp.int32, (n, n), 1)
        wanted = ((i & (cols * n_s - 1)) // cols) * per + (i & (cols - 1)) * 8 + i // (cols * n_s)
        order[...] = jnp.where(j == wanted, 1.0, 0.0).astype(BF16)
        i = lax.broadcasted_iota(jnp.int32, (split, split), 0)
        j = lax.broadcasted_iota(jnp.int32, (split, split), 1)
        swap[...] = jnp.where(j == (i & (z - 1)) * 4 + (i // z & 1) * 2 + i // (2 * z), 1.0, 0.0).astype(BF16)
        fold_zeros(wt, z, channels)
    with jax.named_scope("loadt"):
        small[1].wait()
        parts = fold_parts(mw_ref)
        for load in taps:
            load.wait()
    with jax.named_scope("fold"):
        fold_taps(cwt, parts, wt, z, range(K))
    with jax.named_scope("loadx"):
        small[0].wait()
        for load in xs[0]:
            load.wait()
    with jax.named_scope("act0"):
        gain = gain_ref[...].reshape(1, channels) * (0.5 * channels**0.5)
        activate(0, half // 2 + 2)
        for load in later:
            load.start()
    with jax.named_scope("conv0"):
        convolve(0)
        pack(0)
    with jax.named_scope("load1"):
        small[2].wait()
        small[3].wait()
        for load in xs[1]:
            load.wait()
    ahead = (s < 2).astype(jnp.int32) + ((s == 0) & (t == 0)).astype(jnp.int32)
    after = (ahead > 0).astype(jnp.int32)
    block = 128

    @pl.loop(0, 2)
    def _(turn):
        @pl.when(turn == after)
        def _():
            with jax.named_scope("barrierwait"):
                pl.semaphore_wait(barrier, expect)
            with jax.named_scope("send0"):
                send(0)

        @pl.when(turn == 0)
        def _():
            with jax.named_scope("conv1"):
                activate(half // 2 + 2, half + 2)
                convolve(1)
                pack(1)

        @pl.when(turn == after)
        def _():
            with jax.named_scope("send1"):
                send(1)

        @pl.when(turn == (ahead == 0).astype(jnp.int32))
        def _():
            with jax.named_scope("loadw"):
                for load in later:
                    load.wait()
            with jax.named_scope("prep"):
                bias_row[...] = fold_bias(mw_ref, cb_ref, mb_ref)
                b = pb_ref[...] + xb_ref[...]
                b = b - jnp.sum(b, axis=-1, keepdims=True) * (1.0 / width)
                scaled = scale_ref[...] + 1.0
                center[...] = scaled
                step = 512
                whole = None
                for k in range(0, width, step):
                    at = slice(k, k + step)
                    part = jnp.dot(swap[...], lat_w[:, at], preferred_element_type=F32)
                    both[split : 2 * split, at] = part.astype(BF16)
                    whole = part if whole is None else whole + part
                lat_mean = jnp.sum(whole, axis=-1, keepdims=True) * (1.0 / width)
                late_mean[...] = jnp.broadcast_to(lat_mean, late_mean.shape)
                for k in range(0, width, step):
                    at = slice(k, k + step)
                    part = both[split : 2 * split, at].astype(F32) - lat_mean
                    high, low = halves(part * scaled[:, at])
                    late_ref[:split, at] = high
                    late_ref[split:, at] = low
                high = b.astype(BF16).astype(F32)
                mid = (b - high).astype(BF16).astype(F32)
                row = lax.broadcasted_iota(jnp.int32, (16, width), 0)
                picked = jnp.where(row == 1, high, jnp.where(row == 2, mid, jnp.where(row == 3, b - high - mid, 1.0)))
                both[depth : depth + 16, :] = jnp.where(row < 6, picked, 0.0).astype(BF16)
                noise = own[...].astype(F32).T
                x_early[:, : 2 * split] = jnp.concatenate([noise, jnp.zeros_like(noise)], axis=1).astype(BF16)

        @pl.when(turn == (ahead < 2).astype(jnp.int32))
        def _():
            with jax.named_scope("gram"):
                for part in range(2):
                    at = slice(part * (width // 2), (part + 1) * (width // 2))
                    probe = jnp.concatenate([both[split : 2 * split, at], both[depth : depth + 16, at]], axis=0)
                    gram[part] = nt(probe, both[:depth, at])
                square = gram[0] + gram[1]
                sums = square[split:]
                wmean = sums[0:1] * (1.0 / width)
                cross = (sums[1:2] + sums[2:3] + sums[3:4]) * 2.0
                high, low = halves(square[:split] - late_mean[:, :1] * (wmean * width))
                own_gram[:split, :] = high[:, : 2 * split]
                own_gram[split:, :] = low[:, : 2 * split]
                pair_high = jnp.concatenate([high, high], axis=0)
                pair_low = jnp.concatenate([low, low], axis=0)
                for k in range(0, tokens, block):
                    at = slice(k, k + block)
                    x = x_early[at, :]
                    y = nt(x, pair_high) + nt(x, pair_low)
                    mean = jnp.sum(x.astype(F32) * wmean, axis=-1, keepdims=True)
                    high = mean.astype(BF16).astype(F32)
                    mid = (mean - high).astype(BF16).astype(F32)
                    spot = lax.broadcasted_iota(jnp.int32, (block, 128), 1) - split
                    extra = jnp.where(spot == 0, -high, jnp.where(spot == 4, -mid, high + mid - mean))
                    extra = jnp.where((spot > 0) & (spot < 4), 1.0, extra)
                    x = x[:, : 2 * split].astype(F32)
                    x_early[at, : 2 * split] = jnp.where((spot >= 0) & (spot < 6), extra, x).astype(BF16)
                    base[1, at, :] = 2.0 * y + cross[:, : 2 * split]

    with jax.named_scope("early"):
        step = 256
        for k in range(0, width, step):
            at = slice(k, k + step)
            right = jnp.concatenate(
                [both[:split, at], both[depth : depth + 16, at], both[: split - 16, at], both[2 * split : depth, at]],
                axis=0,
            )
            part = jnp.dot(x_early[...], right, preferred_element_type=F32)
            early_ref[:, at] = part * center[:, at]
            square = part * part
            square = square[:, :128] + square[:, 128:]
            base[0] = square if k == 0 else base[0] + square

        @pl.when(jnp.logical_not(carried))
        def _():
            got[1] = jnp.zeros(got.shape[1:], BF16)

    def drain(slot, own_piece):
        total = (frames if slot == 0 else reach - frames) * chunks
        for ci in range(n_c):
            less = own_piece & (c == ci)

            @pl.when(less)
            def _():
                part = msg.at[: total - 1]
                pltpu.make_async_copy(part, part, s_sem.at[slot, ci]).wait()

            @pl.when(jnp.logical_not(less))
            def _():
                part = msg.at[:total]
                pltpu.make_async_copy(part, part, s_sem.at[slot, ci]).wait()

    with jax.named_scope("drain"):
        drain(0, own_main)

        @pl.when(more)
        def _():
            drain(1, own_carry)

    with jax.named_scope("recv"):

        @pl.when(carried)
        def _():
            pltpu.make_async_copy(got.at[1], got.at[1], r_sem.at[1]).wait()

        pltpu.make_async_copy(got.at[0], got.at[0], r_sem.at[0]).wait()

    with jax.named_scope("assemble"):
        odd = lane // (2 * z) % 2 == 1

        def strip(slot, si):
            v = got[slot, si, :per, :].astype(F32)
            parts = [v[k : k + 8] for k in range(0, per, 8)]
            if si > 0:
                parts[0] = parts[0] + jnp.where(odd, 0.0, got[slot, si - 1, per:, :].astype(F32))
            if si < n_s - 1:
                parts[-1] = parts[-1] + jnp.where(odd, got[slot, si + 1, per:, :].astype(F32), 0.0)
            return jnp.concatenate(parts, axis=0)

        strips = [(strip(0, si) + strip(1, si) + bias_row[...]).astype(BF16) for si in range(n_s)]
        placed = jnp.dot(order[...], jnp.concatenate(strips, axis=0), preferred_element_type=F32)
        turned = pltpu.roll(placed, 64, 1)
        low = lax.broadcasted_iota(jnp.int32, (n, 128), 1) < 64
        twice = [jnp.where(low, placed, turned), jnp.where(low, turned, placed)]
        for h in range(2):
            lhs_ref[h * n : (h + 1) * n, :] = twice[h].astype(BF16)

    with jax.named_scope("stats"):
        for k in range(0, tokens, block):
            at = slice(k, k + block)
            x = lhs_ref[at, :]
            y = jnp.dot(x, own_gram[...], preferred_element_type=F32) + base[1, at, :]
            upper = lax.broadcasted_iota(jnp.int32, (block, 128), 1) >= split
            power = jnp.sum(jnp.where(upper, x.astype(F32) * y, 0.0) + base[0, at, :], axis=-1, keepdims=True)
            variance = jnp.maximum(power * (1.0 / width), 0.0)
            inv_ref[at, :] = jnp.broadcast_to(lax.rsqrt(variance + 1e-06), (block, 128))


def write_kernel(lhs, late, early, inv, shift, out, buf, sem):
    width = buf.shape[1]
    wide = 512 if width % 512 == 0 else width
    step = min(wide, 256)
    copies = []
    for k in range(0, width, wide):
        for q in range(k, k + wide, step):
            at = slice(q, q + step)
            part = jnp.dot(lhs[...], late[:, at], preferred_element_type=F32)
            factor = jnp.concatenate([inv[...]] * (step // 128), axis=1)
            buf[:, at] = ((part + early[:, at]) * factor + shift[:, at]).astype(BF16)
        copy = pltpu.make_async_copy(buf.at[:, k : k + wide], out.at[:, k : k + wide], sem.at[k // wide])
        copy.start()
        copies.append(copy)
    for copy in copies:
        copy.wait()


def fast(
    section_input, norm_gain, conv_weight, conv_bias, mean_weight, mean_bias, noisy_tokens,
    mask_tokens, patch_weight, patch_bias, context_weight, context_bias, norm_shift, norm_scale,
):
    frames, height, columns, channels = section_input.shape
    n_c, n_s, n_t = lax.axis_size("cfg"), lax.axis_size("seq"), lax.axis_size("tile")
    z = mean_weight.shape[1]
    tokens, width = noisy_tokens.shape[0], patch_weight.shape[1]
    shard_rows = tokens // (n_s * columns // 2)
    half = height // n_c
    count = half * columns
    chunks = half // 2 // shard_rows
    reach = frames + K - 1
    per = (columns // 2 + 1) * 8
    depth = patch_weight.shape[0] + context_weight.shape[0]
    split = 4 * z
    n = n_s * columns // 2 * 8
    vmem = pl.BlockSpec(memory_space=pltpu.VMEM)
    hbm = pl.BlockSpec(memory_space=pltpu.HBM)
    args = (
        section_input, conv_weight.T, norm_gain, mean_weight.T, conv_bias[None], mean_bias[None],
        noisy_tokens.T, mask_tokens, patch_weight, context_weight, patch_bias[None], context_bias[None],
        norm_scale[None],
    )
    prepared = pl.pallas_call(
        functools.partial(send_kernel, (n_c, n_s, n_t, shard_rows)),
        out_shape=(
            pltpu.VMEM((tokens, 2 * split), BF16),
            pltpu.VMEM((2 * split, width), BF16),
            pltpu.VMEM((tokens, width), F32),
            pltpu.VMEM((tokens, 128), F32),
        ),
        in_specs=[hbm] * len(args),
        out_specs=(vmem,) * 4,
        scratch_shapes=[
            pltpu.VMEM(conv_weight.shape[::-1], BF16),
            pltpu.VMEM((channels,), F32),
            pltpu.VMEM(mean_weight.shape[::-1], F32),
            pltpu.VMEM((1, conv_bias.shape[0]), F32),
            pltpu.VMEM((1, z), F32),
            pltpu.VMEM((1, width), F32),
            pltpu.VMEM((1, width), F32),
            pltpu.VMEM((1, width), F32),
            pltpu.VMEM((16 * z, frames * K * channels), BF16),
            pltpu.VMEM((frames, half + 2, columns, channels), BF16),
            pltpu.VMEM((frames, (half + 2) * columns, channels), F32),
            pltpu.VMEM((frames, count, 128), F32),
            pltpu.VMEM((frames, count, 128), F32),
            pltpu.VMEM((reach * chunks, per, 128), BF16),
            pltpu.VMEM((2, n_s, per, 128), BF16),
            pltpu.VMEM((split, width), BF16),
            pltpu.VMEM((depth + 16, width), BF16),
            pltpu.VMEM(noisy_tokens.shape[::-1], BF16),
            pltpu.VMEM((2, split + 16, depth), F32),
            pltpu.VMEM((2 * split, 2 * split), BF16),
            pltpu.VMEM((n, n), BF16),
            pltpu.VMEM((split, split), BF16),
            pltpu.VMEM((1, 128), F32),
            pltpu.VMEM((1, width), F32),
            pltpu.VMEM((split, 128), F32),
            pltpu.VMEM((tokens, depth), BF16),
            pltpu.VMEM((2, tokens, 128), F32),
            pltpu.SemaphoreType.DMA((19,)),
            pltpu.SemaphoreType.DMA((2, n_c)),
            pltpu.SemaphoreType.DMA((2,)),
        ],
        compiler_params=pltpu.CompilerParams(
            collective_id=0, has_side_effects=True, vmem_limit_bytes=32 * 2**20
        ),
        name="send",
    )(*(pltpu.with_memory_space_constraint(v, pltpu.HBM) for v in args))
    return pl.pallas_call(
        write_kernel,
        out_shape=jax.ShapeDtypeStruct((tokens, width), BF16),
        in_specs=[vmem] * 5,
        out_specs=hbm,
        scratch_shapes=[pltpu.VMEM((tokens, width), BF16), pltpu.SemaphoreType.DMA((max(1, width // 512),))],
        compiler_params=pltpu.CompilerParams(vmem_limit_bytes=24 * 2**20),
        name="write",
    )(*prepared, norm_shift[None])


def choose(*args):
    n_c, n_s, n_t = lax.axis_size("cfg"), lax.axis_size("seq"), lax.axis_size("tile")
    frames, height, columns, _ = args[0].shape
    rows = args[6].shape[0] // (n_s * columns // 2)
    fits = columns == 8 and args[4].shape[1] == 16 and frames == 2 and rows == 16
    fits = fits and height // n_c == 4 * rows
    return fast(*args) if fits else body(*args)


def solution(mesh):
    placed = (P("tile", None, "seq", None),) + (P(),) * 5
    placed = placed + (P(("seq", "tile"), None),) * 2 + (P(),) * 6
    return jax.shard_map(
        choose, mesh=mesh, in_specs=placed, out_specs=P(("seq", "tile"), None), check_vma=False
    )
```

```python
import functools

import jax
import jax.numpy as jnp
from jax import lax
from jax.experimental import pallas as pl
from jax.experimental.pallas import tpu as pltpu
from jax.sharding import PartitionSpec as P

K = 3
MESH = pl.DeviceIdType.MESH
F32 = jnp.float32
BF16 = jnp.bfloat16


def ones_where(shape, test):
    i = lax.broadcasted_iota(jnp.int32, shape, 0)
    j = lax.broadcasted_iota(jnp.int32, shape, 1)
    return jnp.where(test(i, j), 1.0, 0.0)


def nt(x, y):
    return lax.dot_general(x, y, (((1,), (1,)), ((), ())), preferred_element_type=F32)


def fold_weights(cw_ref, mw_ref, wt):
    z, zo = mw_ref.shape
    mw = mw_ref[...]
    high = mw.astype(BF16)
    low = (mw - high.astype(F32)).astype(BF16)
    spread = ones_where((4 * z, z), lambda i, j: i % z == j).astype(BF16)
    copier = ones_where((zo, K * zo), lambda i, j: j % zo == i).astype(BF16)

    def right_slot(i, j):
        slot, e = i // z, j // zo
        return ((slot == 0) & (e == 1)) | ((slot == 2) & (e == 0)) | ((slot == 3) & (e == 2))

    keep = ones_where((4 * z, K * zo), right_slot)
    parts = []
    for part in (high, low):
        tall = jnp.dot(spread, part, preferred_element_type=F32).astype(BF16)
        parts.append((jnp.dot(tall, copier, preferred_element_type=F32) * keep).astype(BF16))
    parts = jnp.concatenate(parts, axis=0)
    nothing = jnp.zeros((z, wt.shape[2]), BF16)
    for a in range(K):
        for b in range(K):
            at = (a * K + b) * K * zo
            rhs = cw_ref[at : at + K * zo, :]
            res = jnp.dot(parts, rhs, preferred_element_type=F32)
            res = (res[: 4 * z] + res[4 * z :]).astype(BF16)
            for f in range(2):
                for slot in range(4):
                    row = slot * 4 * z + (f + 2 - a) * z
                    wt[f * K + b, row : row + z, :] = res[slot * z : (slot + 1) * z]
    for b in range(K):
        for slot in range(4):
            row = slot * 4 * z
            wt[b, row + 3 * z : row + 4 * z, :] = nothing
            wt[K + b, row : row + z, :] = nothing


def fold_bias(mw_ref, cb_ref, mb_ref):
    z = mw_ref.shape[0]
    copier = ones_where((128, z), lambda i, j: i % z == j)
    exact = functools.partial(
        lax.dot_general, dimension_numbers=(((1,), (1,)), ((), ())),
        precision=lax.Precision.HIGHEST, preferred_element_type=F32,
    )
    return exact(exact(cb_ref[...], mw_ref[...]) + mb_ref[...], copier)


def head_kernel(
    sizes, x_hbm, cw_ref, gain_ref, mw_ref, cb_ref, mb_ref, out_ref,
    wt, xin, actf, acc, edge, pk, rs_send, ls_send, ca_send, rs_got, ls_got, ca_got, patch,
    in_sem, s1_sem, r1_sem, s2_sem, r2_sem,
):
    n_c, n_s, n_t, shard_rows = sizes
    c, s, t = lax.axis_index("cfg"), lax.axis_index("seq"), lax.axis_index("tile")
    frames, height, columns, channels = x_hbm.shape
    half = height // n_c
    pairs = half // 2
    z = 16
    chunks = pairs // shard_rows
    chunk_tokens = shard_rows * (columns // 2)

    def dev(ci, si, ti):
        return {"cfg": ci, "seq": si, "tile": ti}

    load = pltpu.make_async_copy(
        x_hbm.at[:, pl.ds(c * (half - 1), half + 1)],
        xin.at[:, pl.ds(1 - c, half + 1)],
        in_sem,
    )
    load.start()

    barrier = pltpu.get_barrier_semaphore()
    links = [(1, 0), (-1, 0), (0, 1), (1, 1), (-1, 1)]

    def there(ds, dt, sign):
        si, ti = s + sign * ds, t + sign * dt
        return (si >= 0) & (si < n_s) & (ti >= 0) & (ti < n_t), si, ti

    expect = jnp.int32(0)
    for ds, dt in links:
        ok, si, ti = there(ds, dt, -1)

        @pl.when(ok)
        def _():
            pl.semaphore_signal(barrier, inc=1, device_id=dev(c, si, ti), device_id_type=MESH)

        ok, _, _ = there(ds, dt, 1)
        expect = expect + ok.astype(jnp.int32)

    first = (s * n_t + t) * shard_rows
    src_t = first // (height // 2) // frames
    src_c = first % (height // 2) // pairs
    for si in range(n_s):
        mine = (src_c == c) & (src_t == t) & (s == si)

        @pl.when(jnp.logical_not(mine))
        def _():
            pl.semaphore_signal(barrier, inc=1, device_id=dev(src_c, si, src_t), device_id_type=MESH)

    own = (src_c == c) & (src_t == t)
    expect = expect + frames * chunks * n_c - own.astype(jnp.int32)

    fold_weights(cw_ref, mw_ref, wt)
    bias = fold_bias(mw_ref, cb_ref, mb_ref)

    zero_row = jnp.zeros((frames, 1, columns, channels), BF16)

    @pl.when(c == 0)
    def _():
        xin[:, 0:1] = zero_row

    @pl.when(c == n_c - 1)
    def _():
        xin[:, half + 1 : half + 2] = zero_row

    load.wait()
    gain = gain_ref[...].reshape(1, channels)
    step_rows = 6 if (half + 2) % 6 == 0 else 2
    for f in range(frames):

        @pl.loop(0, (half + 2) // step_rows)
        def _(r):
            v = xin[f, pl.ds(r * step_rows, step_rows)].astype(F32)
            v = v.reshape(step_rows * columns, channels)
            energy = jnp.sum(v * v, axis=-1, keepdims=True) * (1.0 / channels)
            v = v * lax.rsqrt(energy + 1e-06) * gain
            v = v / (1.0 + jnp.exp(-v))
            at = pl.multiple_of(r * (step_rows * columns), step_rows * columns)
            actf[f, pl.ds(at, step_rows * columns), :] = v

    rows = half * columns
    for m in range(2):
        lo = m * (rows // 2)
        total = None
        for f in range(frames):
            for b in range(K):
                lhs = actf[f, lo + b * columns : lo + b * columns + rows // 2, :].astype(BF16)
                term = nt(lhs, wt[f * K + b])
                total = term if total is None else total + term
        acc[lo : lo + rows // 2, :] = total[:, :128]
        edge[lo : lo + rows // 2, :] = total[:, 128:]

    q = edge[...]
    w_at = lax.broadcasted_iota(jnp.int32, (rows, 128), 0) % columns
    right = jnp.where(w_at == 0, 0.0, pltpu.roll(q, 1, 0))
    left = jnp.where(w_at == columns - 1, 0.0, pltpu.roll(q, rows - 1, 0))
    acc[...] = acc[...] + right + pltpu.roll(left, 64, 1)
    rs_send[...] = edge[pl.ds(columns - 1, half, stride=columns), :].astype(BF16)
    ls_send[...] = edge[pl.ds(0, half, stride=columns), :].astype(BF16)
    quarter = rows // 4
    lane = lax.broadcasted_iota(jnp.int32, (quarter, 128), 1)
    packed = jnp.zeros((quarter, 128), F32)
    for k in range(4):
        part = pltpu.roll(acc[k * quarter : (k + 1) * quarter, :], (k * 32 + 128 - 32) % 128, 1)
        packed = jnp.where(lane // 32 == k, part, packed)
    ca_send[...] = packed.astype(BF16)

    pl.semaphore_wait(barrier, expect)

    bufs = {1: (rs_send, rs_got), -1: (ls_send, ls_got), 0: (ca_send, ca_got)}

    def link_copy(i, sign):
        ds, dt = links[i]
        ok, si, ti = there(ds, dt, sign)
        src, dst = bufs[ds]
        if ds != 0:
            dst = dst.at[dt]
        return ok, pltpu.make_async_remote_copy(
            src_ref=src, dst_ref=dst, send_sem=s1_sem.at[i], recv_sem=r1_sem.at[i],
            device_id=dev(c, si, ti), device_id_type=MESH,
        )

    for i in (2, 3, 4, 0, 1):
        ok, copy = link_copy(i, 1)

        @pl.when(ok)
        def _():
            copy.start()

    for i in (0, 1, 3, 4, 2):
        ds, dt = links[i]
        ok, copy = link_copy(i, -1)

        @pl.when(ok)
        def _():
            copy.wait_recv()
            if ds == 0:
                got = ca_got[...].astype(F32)
                for k in range(4):
                    acc[k * quarter : (k + 1) * quarter, :] += pltpu.roll(got, (128 - 32 * k) % 128, 1)
            else:
                got = bufs[ds][1][dt].astype(F32)
                turn = (128 - 32 * dt - (64 if ds < 0 else 0)) % 128
                if turn:
                    got = pltpu.roll(got, turn, 1)
                at = pl.ds(0 if ds > 0 else columns - 1, half, stride=columns)
                acc[at, :] = acc[at, :] + got

    total = acc[...] + bias
    by_row = total.reshape(pairs, 2, columns, 128)
    even = by_row[:, 0].reshape(pairs * columns, 128)
    odd = by_row[:, 1].reshape(pairs * columns, 128)
    lane = lax.broadcasted_iota(jnp.int32, (pairs * columns, 128), 1)
    mixed = jnp.where(
        lane < 16, even,
        jnp.where(
            lane < 32, pltpu.roll(odd, 16, 1),
            jnp.where(lane < 48, pltpu.roll(even, 16, 1), pltpu.roll(odd, 32, 1)),
        ),
    )
    pk[...] = mixed
    tokens = pairs * columns // 2
    left_half = pk[pl.ds(0, tokens, stride=2), :]
    right_half = pk[pl.ds(1, tokens, stride=2), :]
    lane = lax.broadcasted_iota(jnp.int32, (tokens, 128), 1)
    for f in range(frames):
        one = left_half if f == 0 else pltpu.roll(left_half, 128 - 32 * f, 1)
        two = pltpu.roll(right_half, (32 - 32 * f) % 128, 1) if f != 1 else right_half
        both = jnp.where(lane < 32, one, two)
        for m in range(chunks):
            patch[f * chunks + m] = both[m * chunk_tokens : (m + 1) * chunk_tokens, :64].astype(BF16)

    def patch_copy(f, m, ci):
        shard = ((t * frames + f) * (height // 2) + c * pairs) // shard_rows + m
        si, ti = shard // n_t, shard % n_t
        mine = (si == s) & (ti == t) & (c == ci)
        piece = f * chunks + m
        local = pltpu.make_async_copy(patch.at[piece], out_ref.at[s], r2_sem.at[s])
        away = pltpu.make_async_remote_copy(
            src_ref=patch.at[piece], dst_ref=out_ref.at[s],
            send_sem=s2_sem.at[piece * n_c + ci], recv_sem=r2_sem.at[s],
            device_id=dev(ci, si, ti), device_id_type=MESH,
        )
        return mine, local, away

    every = [(f, m, ci) for f in range(frames) for m in range(chunks) for ci in range(n_c)]
    for item in every:
        mine, local, away = patch_copy(*item)

        @pl.when(mine)
        def _():
            local.start()

        @pl.when(jnp.logical_not(mine))
        def _():
            away.start()

    for si in range(n_s):
        pltpu.make_async_copy(patch.at[0], out_ref.at[si], r2_sem.at[si]).wait()
    for i in range(5):
        ok, copy = link_copy(i, 1)

        @pl.when(ok)
        def _():
            copy.wait_send()

    for item in every:
        mine, _, away = patch_copy(*item)

        @pl.when(jnp.logical_not(mine))
        def _():
            away.wait_send()


def tail_kernel(noisy, mask, lat, pw, cw, pb, cb, shift, scale, out, comb, both, inv_ref, mean_ref, sems):
    split = lat.shape[-1]
    width = comb.shape[1]
    step = 512
    z = split // 4

    @pl.when(pl.program_id(0) == 0)
    def _():
        upper = pltpu.make_async_copy(pw, both.at[:split], sems.at[0])
        lower = pltpu.make_async_copy(cw, both.at[split:], sems.at[1])
        upper.start()
        lower.start()
        upper.wait()
        lower.wait()

    parts = comb.shape[0] // out.shape[0]

    @pl.when(pl.program_id(0) % parts == 0)
    def _():
        perm = ones_where(
            (split, split), lambda i, j: j == (i % z) * 4 + (i // z % 2) * 2 + i // (2 * z)
        ).astype(BF16)
        if len(lat.shape) == 3:
            strips, per, _ = lat.shape
            tokens = lat[...].reshape(strips * per, split)
            n, cols = strips * per, 4
            order = ones_where(
                (n, n),
                lambda i, j: j == (i // cols % strips) * per + i // (cols * strips) * cols + i % cols,
            ).astype(BF16)
            tokens = jnp.dot(order, tokens, preferred_element_type=F32).astype(BF16)
        else:
            tokens = lat[...]
        tokens = jnp.dot(tokens, perm, preferred_element_type=F32)
        own = noisy[...].astype(F32).T
        lhs = jnp.concatenate([own, tokens, mask[...].astype(F32)], axis=1).astype(BF16)
        total = None
        for k in range(0, width, step):
            at = slice(k, k + step)
            part = jnp.dot(lhs, both[:, at], preferred_element_type=F32)
            part = part + (pb[:, at] + cb[:, at])
            comb[:, at] = part
            term = jnp.sum(part, axis=-1, keepdims=True)
            total = term if total is None else total + term
        mean = total * (1.0 / width)
        square = None
        for k in range(0, width, step):
            d = comb[:, k : k + step] - mean
            term = jnp.sum(d * d, axis=-1, keepdims=True)
            square = term if square is None else square + term
        mean_ref[...] = jnp.broadcast_to(mean, mean_ref.shape)
        inv_ref[...] = jnp.broadcast_to(lax.rsqrt(square * (1.0 / width) + 1e-06), inv_ref.shape)

    rows = out.shape[0]
    mine = pl.ds(pl.multiple_of(pl.program_id(0) % parts * rows, rows), rows)
    mean, inv = mean_ref[mine, :1], inv_ref[mine, :1]
    for k in range(0, width, step):
        at = slice(k, k + step)
        out[:, at] = ((comb[mine, at] - mean) * inv * (1.0 + scale[:, at]) + shift[:, at]).astype(BF16)


def body(
    section_input, norm_gain, conv_weight, conv_bias, mean_weight, mean_bias, noisy_tokens,
    mask_tokens, patch_weight, patch_bias, context_weight, context_bias, norm_shift, norm_scale,
):
    frames, height, columns, channels = section_input.shape
    n_c, n_s, n_t = lax.axis_size("cfg"), lax.axis_size("seq"), lax.axis_size("tile")
    z = mean_weight.shape[1]
    tokens = noisy_tokens.shape[0]
    shard_rows = tokens // (n_s * columns // 2)
    half = height // n_c
    rows = half * columns
    chunks = half // 2 // shard_rows
    chunk_tokens = shard_rows * (columns // 2)
    vmem = pl.BlockSpec(memory_space=pltpu.VMEM)
    arrived = pl.pallas_call(
        functools.partial(head_kernel, (n_c, n_s, n_t, shard_rows)),
        out_shape=jax.ShapeDtypeStruct((n_s, chunk_tokens, 4 * z), BF16),
        in_specs=[pl.BlockSpec(memory_space=pltpu.HBM)] + [vmem] * 5,
        out_specs=vmem,
        scratch_shapes=[
            pltpu.VMEM((frames * K, 16 * z, channels), BF16),
            pltpu.VMEM((frames, half + 2, columns, channels), BF16),
            pltpu.VMEM((frames, (half + 2) * columns, channels), F32),
            pltpu.VMEM((rows, 128), F32),
            pltpu.VMEM((rows, 128), F32),
            pltpu.VMEM((rows // 2, 128), F32),
            pltpu.VMEM((half, 128), BF16),
            pltpu.VMEM((half, 128), BF16),
            pltpu.VMEM((rows // 4, 128), BF16),
            pltpu.VMEM((2, half, 128), BF16),
            pltpu.VMEM((2, half, 128), BF16),
            pltpu.VMEM((rows // 4, 128), BF16),
            pltpu.VMEM((frames * chunks, chunk_tokens, 4 * z), BF16),
            pltpu.SemaphoreType.DMA,
            pltpu.SemaphoreType.DMA((5,)),
            pltpu.SemaphoreType.DMA((5,)),
            pltpu.SemaphoreType.DMA((frames * chunks * n_c,)),
            pltpu.SemaphoreType.DMA((n_s,)),
        ],
        compiler_params=pltpu.CompilerParams(collective_id=0, has_side_effects=True),
        name="head",
    )(
        section_input, conv_weight.T, norm_gain, mean_weight.T, conv_bias[None], mean_bias[None]
    )
    width = patch_weight.shape[1]
    block = min(tokens, 256)
    per = block // n_s
    if per % 16 == 0 and columns == 8:
        lat = arrived
        lat_spec = pl.BlockSpec((n_s, per, 4 * z), lambda i: (0, i // parts, 0))
    else:
        lat = arrived.reshape(n_s, shard_rows, columns // 2, 4 * z).transpose(1, 0, 2, 3)
        lat = lat.reshape(tokens, 4 * z)
        lat_spec = pl.BlockSpec((block, 4 * z), lambda i: (i // parts, 0))
    parts = 2 if block % 32 == 0 else 1
    tok = lambda n: pl.BlockSpec((block, n), lambda i: (i // parts, 0))
    full = lambda a: pl.BlockSpec(a.shape, lambda i: (0, 0))
    hbm = pl.BlockSpec(memory_space=pl.ANY)
    depth = patch_weight.shape[0] + context_weight.shape[0]
    vecs = [v[None] for v in (patch_bias, context_bias, norm_shift, norm_scale)]
    return pl.pallas_call(
        tail_kernel,
        out_shape=jax.ShapeDtypeStruct((tokens, width), BF16),
        grid=(tokens // block * parts,),
        in_specs=[
            pl.BlockSpec((noisy_tokens.shape[1], block), lambda i: (0, i // parts)),
            tok(mask_tokens.shape[1]), lat_spec, hbm, hbm,
        ]
        + [full(v) for v in vecs],
        out_specs=pl.BlockSpec((block // parts, width), lambda i: (i, 0)),
        scratch_shapes=[
            pltpu.VMEM((block, width), F32),
            pltpu.VMEM((depth, width), BF16),
            pltpu.VMEM((block, 128), F32),
            pltpu.VMEM((block, 128), F32),
            pltpu.SemaphoreType.DMA((2,)),
        ],
        name="tail",
    )(noisy_tokens.T, mask_tokens, lat, patch_weight, context_weight, *vecs)


def fold_parts(mw_ref):
    z, zo = mw_ref.shape
    wide = jnp.concatenate([mw_ref[...]] * K, axis=1)
    tap = lax.broadcasted_iota(jnp.int32, wide.shape, 1) // zo
    tall = jnp.concatenate([jnp.where(tap == e, wide, 0.0) for e in (1, 0, 2)], axis=0)
    high = tall.astype(BF16).astype(F32)
    return jnp.concatenate([high, tall - high], axis=1).astype(BF16)


def fold_taps(cw_ref, parts, wt, z, outer):
    channels = cw_ref.shape[1]
    size = parts.shape[1] // 2
    for a in outer:
        for b in range(K):
            at = (a * K + b) * size
            tap = cw_ref[at : at + size, :]
            res = jnp.dot(parts, jnp.concatenate([tap, tap], axis=0), preferred_element_type=F32)
            res = res.astype(BF16)
            for f in range(2):
                for k, slot in enumerate((0, 2, 3)):
                    row = slot * 4 * z + (f + 2 - a) * z
                    wt[row : row + z, (f * K + b) * channels : (f * K + b + 1) * channels] = res[
                        k * z : (k + 1) * z
                    ]


def fold_zeros(wt, z, channels):
    deep = K * channels
    for slot in range(4):
        row = slot * 4 * z
        if slot == 1:
            wt[row : row + 4 * z, :] = jnp.zeros((4 * z, 2 * deep), BF16)
        else:
            wt[row + 3 * z : row + 4 * z, :deep] = jnp.zeros((z, deep), BF16)
            wt[row : row + z, deep:] = jnp.zeros((z, deep), BF16)


def halves(v):
    high = v.astype(BF16)
    return high, (v - high.astype(F32)).astype(BF16)


def send_kernel(
    sizes, x_hbm, cw_hbm, gain_hbm, mw_hbm, cb_hbm, mb_hbm, noisy_hbm, mask_hbm, pw_hbm, xw_hbm, pb_hbm,
    xb_hbm, scale_hbm, lhs_ref, late_ref, early_ref, own_gram, base,
    cwt, gain_ref, mw_ref, cb_ref, mb_ref, pb_ref, xb_ref, scale_ref, wt, xin, actf, cen, edge, msg, got,
    lat_w, both, own, gram, order, swap, bias_row, center, late_mean, x_early, in_sem, s_sem, r_sem,
):
    n_c, n_s, n_t, shard_rows = sizes
    c, s, t = lax.axis_index("cfg"), lax.axis_index("seq"), lax.axis_index("tile")
    frames, height, columns, channels = x_hbm.shape
    half = height // n_c
    pairs = half // 2
    z = mw_ref.shape[0]
    chunks = pairs // shard_rows
    reach = frames + K - 1
    split = 4 * z
    width = late_ref.shape[1]
    tokens = lhs_ref.shape[0]
    depth = pw_hbm.shape[0] + xw_hbm.shape[0]

    def dev(ci, si, ti):
        return {"cfg": ci, "seq": si, "tile": ti}

    cut = half // 2 + 2
    start = c * (half - 1)
    xs = [
        pltpu.make_async_copy(
            x_hbm.at[:, pl.ds(start + lo, size)], xin.at[:, pl.ds(1 - c + lo, size)], in_sem.at[i]
        )
        for i, (lo, size) in enumerate(((0, cut), (cut, half + 1 - cut)))
    ]
    taps = pltpu.make_async_copy(cw_hbm, cwt, in_sem.at[2])
    small = [
        pltpu.make_async_copy(src, dst, in_sem.at[3 + i])
        for i, (src, dst) in enumerate(
            ((gain_hbm, gain_ref), (mw_hbm, mw_ref), (cb_hbm, cb_ref), (mb_hbm, mb_ref))
        )
    ]
    later = [
        pltpu.make_async_copy(src, dst, in_sem.at[i])
        for i, (src, dst) in enumerate(
            (
                (pb_hbm, pb_ref), (xb_hbm, xb_ref), (scale_hbm, scale_ref), (noisy_hbm, own),
                (mask_hbm, x_early.at[:, 2 * split :]), (xw_hbm.at[:split], lat_w),
                (pw_hbm, both.at[:split]), (xw_hbm.at[split:], both.at[2 * split : depth]),
            )
        )
    ]
    small[1].start()
    taps.start()
    xs[0].start()
    small[0].start()
    xs[1].start()
    small[2].start()
    small[3].start()

    barrier = pltpu.get_barrier_semaphore()
    first = (s * n_t + t) * shard_rows
    frame = first // (height // 2)
    src_t = frame // frames
    src_c = first % (height // 2) // pairs
    carried = (src_t > 0) & (frame % frames < K - 1)
    for si in range(n_s):
        for back in range(2):
            mine = (src_c == c) & (src_t - back == t) & (s == si)
            wanted = jnp.logical_not(mine)
            if back:
                wanted = wanted & carried

            @pl.when(wanted)
            def _():
                pl.semaphore_signal(
                    barrier, inc=1, device_id=dev(src_c, si, src_t - back), device_id_type=MESH
                )

    def place(g, m):
        shard = ((t * frames + g) * (height // 2) + c * pairs) // shard_rows + m
        return shard // n_t, shard % n_t

    own_main = (src_c == c) & (src_t == t)
    own_carry = (src_c == c) & (src_t - 1 == t) & carried
    more = t + 1 < n_t
    expect = frames * chunks * n_c - own_main.astype(jnp.int32)
    rest = (reach - frames) * chunks * n_c - own_carry.astype(jnp.int32)
    expect = expect + jnp.where(more, rest, 0)

    zero_row = jnp.zeros((frames, 1, columns, channels), BF16)

    @pl.when(c == 0)
    def _():
        xin[:, 0:1] = zero_row

    @pl.when(c == n_c - 1)
    def _():
        xin[:, half + 1 : half + 2] = zero_row

    def activate(lo, hi):
        step = 2
        for f in range(frames):
            for r in range(lo, hi, step):
                v = xin[f, r : r + step].astype(F32).reshape(step * columns, channels)
                energy = jnp.sum(v * v, axis=-1, keepdims=True)
                v = v * lax.rsqrt(energy + 1e-06 * channels) * gain
                actf[f, r * columns : (r + step) * columns, :] = v + v * jnp.tanh(v)

    count = half * columns // 2

    def convolve(m):
        lo = m * count
        total = None
        for f in range(frames):
            taps = [actf[f, lo + b * columns : lo + b * columns + count, :].astype(BF16) for b in range(K)]
            term = nt(jnp.concatenate(taps, axis=1), wt[:, f * K * channels : (f + 1) * K * channels])
            total = term if total is None else total + jnp.maximum(term, -3e38)
        cen[lo : lo + count, :] = total[:, :128]
        edge[lo : lo + count, :] = total[:, 128:]

    lane = lax.broadcasted_iota(jnp.int32, (8, 128), 1)
    upper = lane >= 64
    one = lane // z % 2 == 1
    two = lane // z % 4 >= 2

    def pack(m):
        cols = {}
        for a in range(2):
            mids, rights, lefts = [], [], []
            for w in range(columns):
                starts = [((m * shard_rows + h * 8) * 2 + a) * columns + w for h in range(2)]
                c0, c1 = (cen[pl.ds(at, 8, stride=2 * columns), :] for at in starts)
                e0, e1 = (edge[pl.ds(at, 8, stride=2 * columns), :] for at in starts)
                mids.append(jnp.where(upper, pltpu.roll(c1, 64, 1), c0))
                turned = pltpu.roll(jnp.where(upper, e0, e1), 64, 1)
                rights.append(jnp.where(upper, turned, e0))
                lefts.append(jnp.where(upper, e1, turned))
            for w in range(columns):
                v = mids[w]
                if w > 0:
                    v = v + rights[w - 1]
                if w < columns - 1:
                    v = v + lefts[w + 1]
                cols[a, w] = v
            cols[a, columns] = rights[columns - 1]
            cols[a, columns + 1] = lefts[0]
        for j in range(columns // 2 + 1):
            p = [cols[a, 2 * j + b] for b in range(2) for a in range(2)]
            q = [None] * 4
            for k in (0, 2):
                q[k] = jnp.where(one, pltpu.roll(p[k + 1], z, 1), p[k])
                q[k + 1] = jnp.where(one, p[k + 1], pltpu.roll(p[k], 128 - z, 1))
            for k in range(2):
                low = jnp.where(two, pltpu.roll(q[k + 2], 2 * z, 1), q[k])
                high = jnp.where(two, q[k + 2], pltpu.roll(q[k], 128 - 2 * z, 1))
                msg[k * chunks + m, j * 8 : j * 8 + 8, :] = low.astype(BF16)
                msg[(k + 2) * chunks + m, j * 8 : j * 8 + 8, :] = high.astype(BF16)

    def send(m):
        def post(g):
            si, ti = place(g, m)
            here = (si == s) & (ti == t)
            slot = g // frames
            src, dst = msg.at[g * chunks + m], got.at[slot, s]
            for ci in range(n_c):

                @pl.when(here & (c == ci))
                def _():
                    pltpu.make_async_copy(src, dst, r_sem.at[slot]).start()

                @pl.when(jnp.logical_not(here & (c == ci)))
                def _():
                    pltpu.make_async_remote_copy(
                        src_ref=src, dst_ref=dst, send_sem=s_sem.at[slot, ci], recv_sem=r_sem.at[slot],
                        device_id=dev(ci, si, ti), device_id_type=MESH,
                    ).start()

        for g in range(frames):
            post(g)

        @pl.when(more)
        def _():
            for g in range(frames, reach):
                post(g)

    per = columns // 2 * 8
    n = n_s * per
    cols = columns // 2
    with jax.named_scope("tables"):
        i = lax.broadcasted_iota(jnp.int32, (n, n), 0)
        j = lax.broadcasted_iota(jnp.int32, (n, n), 1)
        wanted = ((i & (cols * n_s - 1)) // cols) * per + (i & (cols - 1)) * 8 + i // (cols * n_s)
        order[...] = jnp.where(j == wanted, 1.0, 0.0).astype(BF16)
        i = lax.broadcasted_iota(jnp.int32, (split, split), 0)
        j = lax.broadcasted_iota(jnp.int32, (split, split), 1)
        swap[...] = jnp.where(j == (i & (z - 1)) * 4 + (i // z & 1) * 2 + i // (2 * z), 1.0, 0.0).astype(BF16)
        fold_zeros(wt, z, channels)
    with jax.named_scope("loadt"):
        small[1].wait()
        parts = fold_parts(mw_ref)
        taps.wait()
    with jax.named_scope("fold"):
        fold_taps(cwt, parts, wt, z, range(K))
    with jax.named_scope("loadx"):
        small[0].wait()
        xs[0].wait()
    with jax.named_scope("act0"):
        gain = gain_ref[...].reshape(1, channels) * (0.5 * channels**0.5)
        xs[1].wait()
        small[2].wait()
        small[3].wait()
        for load in later:
            load.start()
        activate(0, half // 2 + 2)
        activate(half // 2 + 2, half + 2)
        convolve(0)
        pack(0)

    after = (s < 2).astype(jnp.int32)
    block = 128

    @pl.loop(0, 2)
    def _(turn):
        @pl.when(turn == after)
        def _():
            with jax.named_scope("barrierwait"):
                pl.semaphore_wait(barrier, expect)
            with jax.named_scope("send0"):
                send(0)

        @pl.when(turn == 0)
        def _():
            with jax.named_scope("conv1"):
                convolve(1)
                pack(1)

        @pl.when(turn == after)
        def _():
            with jax.named_scope("send1"):
                send(1)

        @pl.when(turn == 1 - after)
        def _():
            with jax.named_scope("loadw"):
                for load in later:
                    load.wait()
            with jax.named_scope("prep"):
                bias_row[...] = fold_bias(mw_ref, cb_ref, mb_ref)
                b = pb_ref[...] + xb_ref[...]
                b = b - jnp.sum(b, axis=-1, keepdims=True) * (1.0 / width)
                scaled = scale_ref[...] + 1.0
                center[...] = scaled
                step = 512
                whole = None
                for k in range(0, width, step):
                    at = slice(k, k + step)
                    part = jnp.dot(swap[...], lat_w[:, at], preferred_element_type=F32)
                    both[split : 2 * split, at] = part.astype(BF16)
                    whole = part if whole is None else whole + part
                lat_mean = jnp.sum(whole, axis=-1, keepdims=True) * (1.0 / width)
                late_mean[...] = jnp.broadcast_to(lat_mean, late_mean.shape)
                for k in range(0, width, step):
                    at = slice(k, k + step)
                    part = both[split : 2 * split, at].astype(F32) - lat_mean
                    high, low = halves(part * scaled[:, at])
                    late_ref[:split, at] = high
                    late_ref[split:, at] = low
                high = b.astype(BF16).astype(F32)
                mid = (b - high).astype(BF16).astype(F32)
                row = lax.broadcasted_iota(jnp.int32, (16, width), 0)
                picked = jnp.where(row == 1, high, jnp.where(row == 2, mid, jnp.where(row == 3, b - high - mid, 1.0)))
                both[depth : depth + 16, :] = jnp.where(row < 6, picked, 0.0).astype(BF16)
                noise = own[...].astype(F32).T
                x_early[:, : 2 * split] = jnp.concatenate([noise, jnp.zeros_like(noise)], axis=1).astype(BF16)

        @pl.when(turn == 1)
        def _():
            with jax.named_scope("gram"):
                for part in range(2):
                    at = slice(part * (width // 2), (part + 1) * (width // 2))
                    probe = jnp.concatenate([both[split : 2 * split, at], both[depth : depth + 16, at]], axis=0)
                    gram[part] = nt(probe, both[:depth, at])
                square = gram[0] + gram[1]
                sums = square[split:]
                wmean = sums[0:1] * (1.0 / width)
                cross = (sums[1:2] + sums[2:3] + sums[3:4]) * 2.0
                high, low = halves(square[:split] - late_mean[:, :1] * (wmean * width))
                own_gram[:split, :] = high[:, : 2 * split]
                own_gram[split:, :] = low[:, : 2 * split]
                pair_high = jnp.concatenate([high, high], axis=0)
                pair_low = jnp.concatenate([low, low], axis=0)
                for k in range(0, tokens, block):
                    at = slice(k, k + block)
                    x = x_early[at, :]
                    y = nt(x, pair_high) + nt(x, pair_low)
                    mean = jnp.sum(x.astype(F32) * wmean, axis=-1, keepdims=True)
                    high = mean.astype(BF16).astype(F32)
                    mid = (mean - high).astype(BF16).astype(F32)
                    spot = lax.broadcasted_iota(jnp.int32, (block, 128), 1) - split
                    extra = jnp.where(spot == 0, -high, jnp.where(spot == 4, -mid, high + mid - mean))
                    extra = jnp.where((spot > 0) & (spot < 4), 1.0, extra)
                    x = x[:, : 2 * split].astype(F32)
                    x_early[at, : 2 * split] = jnp.where((spot >= 0) & (spot < 6), extra, x).astype(BF16)
                    base[1, at, :] = 2.0 * y + cross[:, : 2 * split]

    with jax.named_scope("early"):
        step = 256
        for k in range(0, width, step):
            at = slice(k, k + step)
            right = jnp.concatenate(
                [both[:split, at], both[depth : depth + 16, at], both[: split - 16, at], both[2 * split : depth, at]],
                axis=0,
            )
            part = jnp.dot(x_early[...], right, preferred_element_type=F32)
            early_ref[:, at] = part * center[:, at]
            square = part * part
            square = square[:, :128] + square[:, 128:]
            base[0] = square if k == 0 else base[0] + square

        @pl.when(jnp.logical_not(carried))
        def _():
            got[1] = jnp.zeros(got.shape[1:], BF16)

    def drain(slot, own_piece):
        total = (frames if slot == 0 else reach - frames) * chunks
        for ci in range(n_c):
            less = own_piece & (c == ci)

            @pl.when(less)
            def _():
                part = msg.at[: total - 1]
                pltpu.make_async_copy(part, part, s_sem.at[slot, ci]).wait()

            @pl.when(jnp.logical_not(less))
            def _():
                part = msg.at[:total]
                pltpu.make_async_copy(part, part, s_sem.at[slot, ci]).wait()

    with jax.named_scope("drain"):
        drain(0, own_main)

        @pl.when(more)
        def _():
            drain(1, own_carry)

    with jax.named_scope("recv"):

        @pl.when(carried)
        def _():
            pltpu.make_async_copy(got.at[1], got.at[1], r_sem.at[1]).wait()

        pltpu.make_async_copy(got.at[0], got.at[0], r_sem.at[0]).wait()

    with jax.named_scope("assemble"):
        odd = lane // (2 * z) % 2 == 1

        def strip(slot, si):
            v = got[slot, si, :per, :].astype(F32)
            parts = [v[k : k + 8] for k in range(0, per, 8)]
            if si > 0:
                parts[0] = parts[0] + jnp.where(odd, 0.0, got[slot, si - 1, per:, :].astype(F32))
            if si < n_s - 1:
                parts[-1] = parts[-1] + jnp.where(odd, got[slot, si + 1, per:, :].astype(F32), 0.0)
            return jnp.concatenate(parts, axis=0)

        strips = [(strip(0, si) + strip(1, si) + bias_row[...]).astype(BF16) for si in range(n_s)]
        placed = jnp.dot(order[...], jnp.concatenate(strips, axis=0), preferred_element_type=F32)
        turned = pltpu.roll(placed, 64, 1)
        low = lax.broadcasted_iota(jnp.int32, (n, 128), 1) < 64
        twice = [jnp.where(low, placed, turned), jnp.where(low, turned, placed)]
        for h in range(2):
            lhs_ref[h * n : (h + 1) * n, :] = twice[h].astype(BF16)


def write_kernel(lhs, late, early, own_gram, base, shift, out, buf, inv, sem):
    tokens, width = buf.shape
    split = lhs.shape[1] // 2
    block = 128
    upper = lax.broadcasted_iota(jnp.int32, (block, 128), 1) >= split
    for k in range(0, tokens, block):
        at = slice(k, k + block)
        x = lhs[at, :]
        y = jnp.dot(x, own_gram[...], preferred_element_type=F32) + base[1, at, :]
        power = jnp.sum(jnp.where(upper, x.astype(F32) * y, 0.0) + base[0, at, :], axis=-1, keepdims=True)
        variance = jnp.maximum(power * (1.0 / width), 0.0)
        inv[at, :] = jnp.broadcast_to(lax.rsqrt(variance + 1e-06), (block, 128))
    step = 256 if width % 256 == 0 else width
    steps = width // step
    last = 0
    for q in range(steps):
        at = slice(q * step, (q + 1) * step)
        part = jnp.dot(lhs[...], late[:, at], preferred_element_type=F32)
        factor = jnp.concatenate([inv[...]] * (step // 128), axis=1)
        buf[:, at] = ((part + early[:, at]) * factor + shift[:, at]).astype(BF16)
        if q % 2 == 1 or q == steps - 1:
            done = slice(last * step, (q + 1) * step)
            pltpu.make_async_copy(buf.at[:, done], out.at[:, done], sem).start()
            last = q + 1
    pltpu.make_async_copy(buf, out, sem).wait()


def fast(
    section_input, norm_gain, conv_weight, conv_bias, mean_weight, mean_bias, noisy_tokens,
    mask_tokens, patch_weight, patch_bias, context_weight, context_bias, norm_shift, norm_scale,
):
    frames, height, columns, channels = section_input.shape
    n_c, n_s, n_t = lax.axis_size("cfg"), lax.axis_size("seq"), lax.axis_size("tile")
    z = mean_weight.shape[1]
    tokens, width = noisy_tokens.shape[0], patch_weight.shape[1]
    shard_rows = tokens // (n_s * columns // 2)
    half = height // n_c
    count = half * columns
    chunks = half // 2 // shard_rows
    reach = frames + K - 1
    per = (columns // 2 + 1) * 8
    depth = patch_weight.shape[0] + context_weight.shape[0]
    split = 4 * z
    n = n_s * columns // 2 * 8
    vmem = pl.BlockSpec(memory_space=pltpu.VMEM)
    hbm = pl.BlockSpec(memory_space=pltpu.HBM)
    args = (
        section_input, conv_weight.T, norm_gain, mean_weight.T, conv_bias[None], mean_bias[None],
        noisy_tokens.T, mask_tokens, patch_weight, context_weight, patch_bias[None], context_bias[None],
        norm_scale[None],
    )
    prepared = pl.pallas_call(
        functools.partial(send_kernel, (n_c, n_s, n_t, shard_rows)),
        out_shape=(
            pltpu.VMEM((tokens, 2 * split), BF16),
            pltpu.VMEM((2 * split, width), BF16),
            pltpu.VMEM((tokens, width), F32),
            pltpu.VMEM((2 * split, 2 * split), BF16),
            pltpu.VMEM((2, tokens, 128), F32),
        ),
        in_specs=[hbm] * len(args),
        out_specs=(vmem,) * 5,
        scratch_shapes=[
            pltpu.VMEM(conv_weight.shape[::-1], BF16),
            pltpu.VMEM((channels,), F32),
            pltpu.VMEM(mean_weight.shape[::-1], F32),
            pltpu.VMEM((1, conv_bias.shape[0]), F32),
            pltpu.VMEM((1, z), F32),
            pltpu.VMEM((1, width), F32),
            pltpu.VMEM((1, width), F32),
            pltpu.VMEM((1, width), F32),
            pltpu.VMEM((16 * z, frames * K * channels), BF16),
            pltpu.VMEM((frames, half + 2, columns, channels), BF16),
            pltpu.VMEM((frames, (half + 2) * columns, channels), F32),
            pltpu.VMEM((count, 128), F32),
            pltpu.VMEM((count, 128), F32),
            pltpu.VMEM((reach * chunks, per, 128), BF16),
            pltpu.VMEM((2, n_s, per, 128), BF16),
            pltpu.VMEM((split, width), BF16),
            pltpu.VMEM((depth + 16, width), BF16),
            pltpu.VMEM(noisy_tokens.shape[::-1], BF16),
            pltpu.VMEM((2, split + 16, depth), F32),
            pltpu.VMEM((n, n), BF16),
            pltpu.VMEM((split, split), BF16),
            pltpu.VMEM((1, 128), F32),
            pltpu.VMEM((1, width), F32),
            pltpu.VMEM((split, 128), F32),
            pltpu.VMEM((tokens, depth), BF16),
            pltpu.SemaphoreType.DMA((8,)),
            pltpu.SemaphoreType.DMA((2, n_c)),
            pltpu.SemaphoreType.DMA((2,)),
        ],
        compiler_params=pltpu.CompilerParams(
            collective_id=0, has_side_effects=True, vmem_limit_bytes=32 * 2**20
        ),
        name="send",
    )(*(pltpu.with_memory_space_constraint(v, pltpu.HBM) for v in args))
    return pl.pallas_call(
        write_kernel,
        out_shape=jax.ShapeDtypeStruct((tokens, width), BF16),
        in_specs=[vmem] * 6,
        out_specs=hbm,
        scratch_shapes=[pltpu.VMEM((tokens, width), BF16), pltpu.VMEM((tokens, 128), F32), pltpu.SemaphoreType.DMA],
        compiler_params=pltpu.CompilerParams(vmem_limit_bytes=24 * 2**20),
        name="write",
    )(*prepared, norm_shift[None])


def choose(*args):
    n_c, n_s, n_t = lax.axis_size("cfg"), lax.axis_size("seq"), lax.axis_size("tile")
    frames, height, columns, _ = args[0].shape
    rows = args[6].shape[0] // (n_s * columns // 2)
    fits = columns == 8 and args[4].shape[1] == 16 and frames == 2 and rows == 16
    fits = fits and height // n_c == 4 * rows
    return fast(*args) if fits else body(*args)


def solution(mesh):
    placed = (P("tile", None, "seq", None),) + (P(),) * 5
    placed = placed + (P(("seq", "tile"), None),) * 2 + (P(),) * 6
    return jax.shard_map(
        choose, mesh=mesh, in_specs=placed, out_specs=P(("seq", "tile"), None), check_vma=False
    )
```
